256 devices in a mesh: balls: 64 (over y, z, core), heads: 4 (over x).
Axes of the slice: x: 4, y: 4, z: 8, core: 2. Of those that a mesh axis runs over, the one named last changes fastest.
Arguments:
- particles: bfloat16 [131072, 512], P('balls'), may hold values from -9.5 to 9.5
- query_weight: bfloat16 [512, 512], P(None, 'heads'), may hold values from -0.53033009 to 0.53033009
- key_weight: bfloat16 [512, 128], P(None, 'heads'), may hold values from -5.5684659 to 5.5684659
- value_weight: bfloat16 [512, 128], P(None, 'heads'), may hold values from -0.25 to 0.25
- out_weight: bfloat16 [512, 512], replicated, may hold values from -0.25 to 0.25
- up_weight: bfloat16 [512, 2048], replicated, may hold values from -0.25 to 0.25
- down_weight: bfloat16 [2048, 512], replicated, may hold values from -0.125 to 0.125
- rotated_slot: int32 [2048], replicated, may hold values from 0 to 2047, as said below
- selected: int32 [512, 3], replicated, may hold values from 0 to 511, as said below
Outputs:
- layer_out: bfloat16 [131072, 512], P(('balls', 'heads'))
The draws below stay inside these ranges and needn't reach their ends.
Inputs may be any that keep to these rules, and one draw needn't show every extreme that they name: rotated_slot is a permutation of 0 to 2047; of the 32 leaf blocks i * 32 to i * 32 + 31, at most 1 land in the positions j * 32 to j * 32 + 31 for any j, and some pair reaches 1 in every draw. `selected`: each row holds 3 different balls; over the rows i * 8 to i * 8 + 7, at most 1 entries name balls j * 8 to j * 8 + 7 for any j, and this is reached in every draw.
All inputs are finite; a program needn't handle non-finite values.
Results may differ from the reference program's by a relative error of at most 0.012.
The reference program's roundings to bfloat16 on the way (of `normed`, `rotated`, `queries`, `weights`, `attended`, `resid`, `mlp_in` and `hidden`) count: a program that leaves them out, or rounds other values in their place, can miss the bound.
Values may be sent and summed in bfloat16 or wider, within the bound.
A program may use at most 64 MiB of HBM per device.

```python
import math
import jax
import jax.numpy as jnp
from jax import lax

D = 512
QHEADS = 16
KVHEADS = 4
HEAD = 32
FF = 2048
BALL = 256
LEAF = 64
TOPK = 3
BALL_DEV = 8
LEAF_DEV = 32
TOKENS = 131072
BALLS = 512
LEAVES = 2048


def draw_particles(key, part):
    base = jax.random.fold_in(key, 31)
    field = jnp.clip(jax.random.normal(jax.random.fold_in(base, 4), (TOKENS, D), jnp.float32), -6.0, 6.0)
    return field.astype(jnp.bfloat16)


def paired_weights(key):
    base = jax.random.fold_in(key, 53)
    raw_query = jnp.clip(jax.random.normal(jax.random.fold_in(base, 1), (D, QHEADS * HEAD), jnp.float32), -6.0, 6.0) * (2.0 / math.sqrt(D))
    raw_key = jnp.clip(jax.random.normal(jax.random.fold_in(base, 2), (D, KVHEADS * HEAD), jnp.float32), -6.0, 6.0) / math.sqrt(D)
    return (raw_query, raw_key)


def draw_query_weight(key, part):
    raw_query, raw_key = paired_weights(key)
    return raw_query.astype(jnp.bfloat16)


def draw_key_weight(key, part):
    raw_query, raw_key = paired_weights(key)
    return raw_key.astype(jnp.bfloat16)


def draw_rotated_slot(key, part):
    devices = LEAVES // LEAF_DEV
    capacity = (LEAF_DEV + devices - 1) // devices
    count = LEAF_DEV // capacity
    base = jax.random.fold_in(key, 7)
    values = jnp.arange(devices, dtype=jnp.int32)
    random_rank = jax.random.permutation(jax.random.fold_in(base, 1), devices).astype(jnp.int32)
    priority = jnp.where(values == 1, 0, jnp.where(values == devices // 2, 1, jnp.where(values == devices - 1, 2, 3 + random_rank)))
    priority = priority * devices + values
    shifts = jnp.argsort(priority)[:count].astype(jnp.int32)
    order = jax.vmap(lambda sub: jax.random.permutation(sub, LEAF_DEV))(jax.random.split(jax.random.fold_in(base, 2), devices)).astype(jnp.int32)
    landing = jax.vmap(lambda sub: jax.random.permutation(sub, LEAF_DEV))(jax.random.split(jax.random.fold_in(base, 3), devices)).astype(jnp.int32)
    source = jnp.arange(devices, dtype=jnp.int32)[:, None]
    target = (source + shifts[order // capacity]) % devices
    position = target * LEAF_DEV + landing[target, order]
    return position.reshape(LEAVES).astype(jnp.int32)


def draw_selected(key, part):
    devices = BALLS // BALL_DEV
    picks = BALL_DEV * TOPK
    capacity = (picks + devices - 1) // devices
    base = jax.random.fold_in(key, 19)

    def reader(sub, index):
        first, second, third, fourth = jax.random.split(sub, 4)
        shifts = jax.random.permutation(first, devices).astype(jnp.int32)
        flat = jnp.arange(picks, dtype=jnp.int32)
        owner = (index + shifts[flat // capacity]) % devices
        chosen = owner * BALL_DEV + jax.random.randint(second, (picks,), 0, BALL_DEV, dtype=jnp.int32)
        table = chosen.reshape(TOPK, BALL_DEV).T
        table = table[jax.random.permutation(third, BALL_DEV)]
        return table[:, jax.random.permutation(fourth, TOPK)]
    result = jax.vmap(reader)(jax.random.split(jax.random.fold_in(base, 1), devices), jnp.arange(devices, dtype=jnp.int32))
    return result.reshape(BALLS, TOPK).astype(jnp.int32)


def levels(own_key, dims, pieces, smallest, high):
    level, own = 1.0, jax.random.fold_in(own_key, 6)
    for axis_at, shards_of in pieces:
        steps = jnp.exp(jax.random.uniform(jax.random.fold_in(own, axis_at), (shards_of,), jnp.float32, smallest / len(pieces), high / len(pieces)))
        level = level * jnp.repeat(steps, dims[axis_at] // shards_of).reshape([-1 if axis == axis_at else 1 for axis in range(len(dims))])
    return level


def normal_values(stream_key, shape, scale, reach, cuts=(), kind=jnp.bfloat16):
    entries = scale * jax.random.normal(stream_key, shape, jnp.float32)
    if cuts:
        entries = entries * levels(stream_key, shape, cuts, -0.22, 0.18)
    return jnp.clip(entries, -reach, reach).astype(kind)


def setup_inputs(seed: int = 0) -> dict:
    key_list = jax.random.split(jax.random.key(seed), 10)
    return {
        "particles": draw_particles(jax.random.fold_in(key_list[9], 71), 0),
        "query_weight": draw_query_weight(jax.random.fold_in(key_list[9], 71), 0),
        "key_weight": draw_key_weight(jax.random.fold_in(key_list[9], 71), 0),
        "value_weight": normal_values(key_list[3], (D, KVHEADS * HEAD), D ** -0.5, 0.25, ((1, 4),)),
        "out_weight": normal_values(key_list[4], (QHEADS * HEAD, D), (QHEADS * HEAD) ** -0.5, 0.25),
        "up_weight": normal_values(key_list[5], (D, FF), D ** -0.5, 0.25),
        "down_weight": normal_values(key_list[6], (FF, D), FF ** -0.5, 0.125),
        "rotated_slot": draw_rotated_slot(jax.random.fold_in(key_list[9], 71), 0),
        "selected": draw_selected(jax.random.fold_in(key_list[9], 71), 0),
    }


def rms_rows(matrix):
    wide = matrix.astype(jnp.float32)
    return (wide * lax.rsqrt(lax.optimization_barrier(jnp.mean(wide * wide, axis=-1, keepdims=True)) + 1e-05)).astype(jnp.bfloat16)

def project(left, right):
    return jnp.dot(left, right, preferred_element_type=jnp.float32).astype(jnp.bfloat16)

def reference(particles, query_weight, key_weight, value_weight, out_weight, up_weight, down_weight, rotated_slot, selected):
    repeat = QHEADS // KVHEADS
    normed = rms_rows(particles)
    key_rows = project(normed, key_weight)
    value_rows = project(normed, value_weight)
    kv_cols = KVHEADS * HEAD
    pooled_keys = (lax.optimization_barrier(jnp.sum(key_rows.reshape(BALLS, BALL, kv_cols), axis=1, dtype=jnp.float32)) / math.sqrt(BALL)).astype(jnp.bfloat16)
    pooled_values = (lax.optimization_barrier(jnp.sum(value_rows.reshape(BALLS, BALL, kv_cols), axis=1, dtype=jnp.float32)) / math.sqrt(BALL)).astype(jnp.bfloat16)
    inverse = jnp.zeros((LEAVES,), jnp.int32).at[rotated_slot].set(jnp.arange(LEAVES, dtype=jnp.int32))

    def permute(matrix):
        columns = matrix.shape[1]
        return matrix.reshape(LEAVES, LEAF, columns)[inverse].reshape(TOKENS, columns)
    rotated = permute(particles)
    rot_normed = permute(normed)
    queries = project(rot_normed, query_weight)
    rot_keys = permute(key_rows)
    rot_values = permute(value_rows)
    ball_keys = key_rows.reshape(BALLS, BALL, KVHEADS, HEAD)
    ball_values = value_rows.reshape(BALLS, BALL, KVHEADS, HEAD)
    pool_k = pooled_keys.reshape(BALLS, KVHEADS, HEAD)
    pool_v = pooled_values.reshape(BALLS, KVHEADS, HEAD)

    def attend(item):
        query_ball, key_ball, value_ball, chosen = item
        chosen_keys = ball_keys[chosen].reshape(TOPK * BALL, KVHEADS, HEAD)
        chosen_values = ball_values[chosen].reshape(TOPK * BALL, KVHEADS, HEAD)
        all_keys = jnp.concatenate([key_ball, pool_k, chosen_keys], axis=0).astype(jnp.float32)
        all_values = jnp.concatenate([value_ball, pool_v, chosen_values], axis=0).astype(jnp.float32)
        scores = jnp.einsum('qgrd,kgd->grqk', query_ball.astype(jnp.float32), all_keys) / math.sqrt(HEAD)
        weights = jax.nn.softmax(scores, axis=-1).astype(jnp.bfloat16)
        result = jnp.einsum('grqk,kgd->qgrd', weights.astype(jnp.float32), all_values)
        return result.reshape(BALL, QHEADS * HEAD).astype(jnp.bfloat16)
    attended = lax.map(attend, (queries.reshape(BALLS, BALL, KVHEADS, repeat, HEAD), rot_keys.reshape(BALLS, BALL, KVHEADS, HEAD), rot_values.reshape(BALLS, BALL, KVHEADS, HEAD), selected)).reshape(TOKENS, QHEADS * HEAD)
    resid = (rotated.astype(jnp.float32) + jnp.dot(attended, out_weight, preferred_element_type=jnp.float32)).astype(jnp.bfloat16)
    mlp_in = rms_rows(resid)
    hidden = jax.nn.gelu(jnp.dot(mlp_in, up_weight, preferred_element_type=jnp.float32)).astype(jnp.bfloat16)
    return (resid.astype(jnp.float32) + jnp.dot(hidden, down_weight, preferred_element_type=jnp.float32)).astype(jnp.bfloat16)
```

```python
import math

import jax
import jax.numpy as jnp
from jax import lax
from jax.experimental import pallas as pl
from jax.experimental.pallas import tpu as pltpu
from jax.sharding import PartitionSpec as P

HEAD = 32
BALL = 256
LEAF = 64
TOPK = 3
NX, NY, NZ, NC = 4, 4, 8, 2
NS = NY * NC
PIECE = LEAF // NX
D = 512
FF = 2048
SCALE = math.log2(math.e) / math.sqrt(HEAD)
NT = (((1,), (1,)), ((), ()))


def rms_rows(matrix):
    wide = matrix.astype(jnp.float32)
    return (wide * lax.rsqrt(jnp.mean(wide * wide, axis=-1, keepdims=True) + 1e-05)).astype(
        jnp.bfloat16
    )


def dot32(left, right, dims=None):
    if dims is None:
        return jnp.dot(left, right, preferred_element_type=jnp.float32)
    return lax.dot_general(left, right, dims, preferred_element_type=jnp.float32)


def kernel(
    tab, p_ref, w_ref, wkvt_ref, wo_hbm, up_hbm, down_hbm, out_ref,
    wo_ref, up_ref, down_ref, w_all,
    leaf_stage, leaf_mid, leaf_recv, rotq, xst, xrecv, rres,
    kv_own, agp1, agp2, agp3, agm1, agm2, agm3, ag4,
    sel_stage, sel_recv, pool_own, pool_z, pool_all,
    kt4, vt4, att_st, att_recv,
    load_sem, ws, wr, lzs, lzr, lss, lsr, xs, xr, rs, rr,
    ags, agr, sss, ssr, pzs, pzr, pss, psr, ats, atr,
):
    b = lax.axis_index("balls")
    h = lax.axis_index("heads")
    y = b // (NZ * NC)
    z = (b // NC) % NZ
    c = b % NC
    k = y * NC + c

    def z_peer(r):
        return {"balls": (y * NZ + (z + r) % NZ) * NC + c, "heads": h}

    def s_peer(o):
        kk = (k + o) % NS
        return {"balls": ((kk // NC) * NZ + z) * NC + kk % NC, "heads": h}

    def x_peer(o):
        return {"balls": b, "heads": (h + o) % NX}

    def remote(src, dst, send, recv, peer):
        return pltpu.make_async_remote_copy(
            src_ref=src, dst_ref=dst, send_sem=send, recv_sem=recv,
            device_id=peer, device_id_type=pl.DeviceIdType.MESH,
        )

    barrier = pltpu.get_barrier_semaphore()

    @pl.loop(1, NZ)
    def _(r):
        pl.semaphore_signal(barrier, 1, device_id=z_peer(r))

    @pl.loop(1, NS)
    def _(o):
        pl.semaphore_signal(barrier, 1, device_id=s_peer(o))

    @pl.loop(1, NX)
    def _(o):
        pl.semaphore_signal(barrier, 1, device_id=x_peer(o))

    loads = [
        pltpu.make_async_copy(wo_hbm, wo_ref, load_sem.at[0]),
        pltpu.make_async_copy(up_hbm, up_ref, load_sem.at[1]),
        pltpu.make_async_copy(down_hbm, down_ref, load_sem.at[2]),
    ]
    for load in loads:
        load.start()

    @pl.loop(0, NZ)
    def _(zd):
        @pl.loop(0, NS)
        def _(kk):
            leaf_stage[zd, kk] = p_ref[tab[zd * NS + kk] * NX + h]

    leaf_mid[z] = leaf_stage[z]
    pl.semaphore_wait(barrier, (NZ - 1) + (NS - 1) + (NX - 1))

    def leaf_z(r):
        return remote(
            leaf_stage.at[(z + r) % NZ], leaf_mid.at[z], lzs.at[r], lzr.at[r], z_peer(r)
        )

    @pl.loop(1, NZ)
    def _(r):
        leaf_z(r).start()

    def weights(o):
        return remote(w_ref, w_all.at[h], ws.at[o], wr.at[o], x_peer(o))

    @pl.loop(1, NX)
    def _(o):
        weights(o).start()

    w_all[h] = w_ref[...]

    ones8 = jnp.ones((8, BALL), jnp.bfloat16)
    row8 = lax.broadcasted_iota(jnp.int32, (8, 128), 0)

    def own_ball(i, pooled):
        rows = p_ref[pl.ds(i * 16, 16)].reshape(BALL, D)
        kvt = dot32(wkvt_ref[...], rms_rows(rows), NT).astype(jnp.bfloat16)
        kv_own[i] = kvt[: 2 * HEAD]
        total = dot32(ones8, kvt, NT) * (1.0 / math.sqrt(BALL))
        return jnp.where(row8 == i, total.astype(jnp.bfloat16).astype(jnp.float32), pooled)

    pooled = lax.fori_loop(0, 8, own_ball, jnp.zeros((8, 128), jnp.float32))
    pool_own[...] = pooled

    half = pl.ds(0, 4)
    rest = pl.ds(4, 4)
    chain_p = [
        remote(kv_own, agp1, ags.at[0], agr.at[0], z_peer(1)),
        remote(agp1, agp2, ags.at[1], agr.at[1], z_peer(1)),
        remote(agp2, agp3, ags.at[2], agr.at[2], z_peer(1)),
        remote(agp3.at[half], ag4.at[half], ags.at[3], agr.at[3], z_peer(1)),
    ]
    chain_m = [
        remote(kv_own, agm1, ags.at[4], agr.at[4], z_peer(NZ - 1)),
        remote(agm1, agm2, ags.at[5], agr.at[5], z_peer(NZ - 1)),
        remote(agm2, agm3, ags.at[6], agr.at[6], z_peer(NZ - 1)),
        remote(agm3.at[rest], ag4.at[rest], ags.at[7], agr.at[7], z_peer(NZ - 1)),
    ]

    def pool_to_z(r):
        return remote(pool_own, pool_z.at[z], pzs.at[r], pzr.at[r], z_peer(r))

    @pl.loop(1, NZ)
    def _(r):
        pool_to_z(r).start()

    chain_p[0].start()
    chain_m[0].start()
    pool_z[z] = pool_own[...]

    def leaf_s(r, o):
        zs = (z + NZ - r) % NZ
        kk = (k + o) % NS
        return remote(
            leaf_mid.at[zs, kk], leaf_recv.at[k * NZ + zs], lss.at[r, o], lsr.at[r, o], s_peer(o)
        )

    @pl.loop(0, NZ)
    def _(r):
        @pl.when(r > 0)
        def _():
            leaf_z(r).wait_recv()

        @pl.loop(1, NS)
        def _(o):
            leaf_s(r, o).start()

        zs = (z + NZ - r) % NZ
        leaf_recv[k * NZ + zs] = leaf_mid[zs, k]

    def pool_to_s(o):
        return remote(pool_z, pool_all.at[k], pss.at[o], psr.at[o], s_peer(o))

    @pl.loop(1, NZ)
    def _(r):
        pool_to_z(r).wait_recv()

    @pl.loop(1, NS)
    def _(o):
        pool_to_s(o).start()

    pool_all[k] = pool_z[...]

    def sel_s(r, o):
        zs = (z + NZ - r) % NZ
        kk = (k + o) % NS
        return remote(
            sel_stage.at[r, kk], sel_recv.at[k * NZ + zs], sss.at[r, o], ssr.at[r, o], s_peer(o)
        )

    def forward(source, r):
        zs = (z + NZ - r) % NZ

        @pl.loop(0, NS)
        def _(kk):
            sel_stage[r, kk] = source[tab[96 + zs * NS + kk]]

        sel_recv[k * NZ + zs] = sel_stage[r, k]

        @pl.loop(1, NS)
        def _(o):
            sel_s(r, o).start()

    forward(kv_own, 0)
    chain_p[0].wait_recv()
    chain_p[1].start()
    chain_m[0].wait_recv()
    chain_m[1].start()
    forward(agp1, 1)
    forward(agm1, 7)

    @pl.loop(0, NZ)
    def _(r):
        @pl.loop(1, NS)
        def _(o):
            leaf_s(r, o).wait_recv()

    @pl.loop(0, 32)
    def _(s):
        rotq[s] = leaf_recv[tab[64 + s]]

    def resid_x(o):
        return remote(
            rotq.at[pl.ds(((h + o) % NX) * 8, 8)], rres.at[h], rs.at[o], rr.at[o], x_peer(o)
        )

    @pl.loop(1, NX)
    def _(o):
        weights(o).wait_recv()

    @pl.loop(0, 4)
    def _(q):
        rows = rms_rows(rotq[pl.ds(q * 8, 8)].reshape(128, D))

        @pl.loop(0, NX)
        def _(g):
            xst[g, pl.ds(pl.multiple_of(q * 128, 128), 128)] = dot32(rows, w_all[g]).astype(
                jnp.bfloat16
            )

    def qkv_x(o):
        return remote(xst.at[(h + o) % NX], xrecv.at[h], xs.at[o], xr.at[o], x_peer(o))

    @pl.loop(1, NX)
    def _(o):
        qkv_x(o).start()

    @pl.loop(1, NX)
    def _(o):
        resid_x(o).start()

    xrecv[h] = xst[h]
    rres[h] = rotq[pl.ds(h * 8, 8)]

    chain_p[1].wait_recv()
    chain_p[2].start()
    chain_m[1].wait_recv()
    chain_m[2].start()
    forward(agp2, 2)
    forward(agm2, 6)
    chain_p[2].wait_recv()
    chain_p[3].start()
    chain_m[2].wait_recv()
    chain_m[3].start()
    forward(agp3, 3)
    forward(agm3, 5)
    chain_p[3].wait_recv()
    chain_m[3].wait_recv()
    forward(ag4, 4)

    kt4[...] = jnp.zeros_like(kt4)
    vt4[...] = jnp.zeros_like(vt4)
    for j in range(4):
        vt4[j, pl.ds(128 + HEAD * j, HEAD), :] = jnp.ones((HEAD, 6 * BALL), jnp.bfloat16)

    eye = (
        lax.broadcasted_iota(jnp.int32, (2 * HEAD, 128), 0)
        == lax.broadcasted_iota(jnp.int32, (2 * HEAD, 128), 1)
    ).astype(jnp.bfloat16)

    def place(block, kvt):
        width = kvt.shape[1]
        for j in range(4):
            kt4[j, pl.ds(HEAD * j, HEAD), pl.ds(block * BALL, width)] = kvt[:HEAD]
            vt4[j, pl.ds(HEAD * j, HEAD), pl.ds(block * BALL, width)] = kvt[HEAD:]

    @pl.loop(1, NS)
    def _(o):
        pool_to_s(o).wait_recv()

    pool_rows = pool_all[...].reshape(2 * BALL, 128).astype(jnp.bfloat16)
    place(1, dot32(eye, pool_rows, NT).astype(jnp.bfloat16))

    @pl.loop(1, NX)
    def _(o):
        qkv_x(o).wait_recv()

    @pl.loop(0, NZ)
    def _(r):
        @pl.loop(1, NS)
        def _(o):
            sel_s(r, o).wait_recv()

    def attend(ball):
        at = pl.ds(pl.multiple_of(ball * 64, 64), 64)
        q = jnp.concatenate([xrecv[g, at, pl.ds(0, 128)] for g in range(NX)], axis=0)
        own = jnp.concatenate([xrecv[g, at, pl.ds(128, 128)] for g in range(NX)], axis=0)
        place(0, dot32(eye, own, NT).astype(jnp.bfloat16))
        for t in range(TOPK):
            place(3 + t, sel_recv[tab[160 + ball * TOPK + t]])

        def head(j, total):
            score = dot32(q, kt4[j])
            top = jnp.max(score, axis=-1, keepdims=True)
            weight = jnp.exp2((score - top) * SCALE).astype(jnp.bfloat16)
            return total + dot32(weight, vt4[j], NT)

        total = lax.fori_loop(0, 4, head, jnp.zeros((BALL, 256), jnp.float32), unroll=2)
        att_st[ball] = (total[:, :128] / total[:, 128:]).astype(jnp.bfloat16)

    def att_x(o):
        return remote(
            att_st.at[pl.ds(((h + o) % NX) * 2, 2)], att_recv.at[h], ats.at[o], atr.at[o], x_peer(o)
        )

    @pl.loop(1, NX + 1)
    def _(o):
        g = (h + o) % NX

        @pl.loop(0, 2)
        def _(i):
            attend(g * 2 + i)

        @pl.when(o < NX)
        def _():
            att_x(o).start()

    att_recv[h] = att_st[pl.ds(h * 2, 2)]

    for load in loads:
        load.wait()

    @pl.loop(1, NX)
    def _(o):
        resid_x(o).wait_recv()

    @pl.loop(1, NX)
    def _(o):
        att_x(o).wait_recv()

    @pl.loop(0, 2)
    def _(i):
        heads = jnp.concatenate([att_recv[g, i] for g in range(NX)], axis=1)
        base = jnp.concatenate(
            [rres[g, pl.ds(i * 4, 4)].reshape(64, D) for g in range(NX)], axis=0
        )
        resid = (base.astype(jnp.float32) + dot32(heads, wo_ref[...])).astype(jnp.bfloat16)
        mlp_in = rms_rows(resid)

        def hidden(f, total):
            cols = pl.ds(pl.multiple_of(f * 512, 512), 512)
            inner = jax.nn.gelu(dot32(mlp_in, up_ref[:, cols])).astype(jnp.bfloat16)
            return total + dot32(inner, down_ref[cols, :])

        done = lax.fori_loop(0, FF // 512, hidden, resid.astype(jnp.float32))
        done = done.astype(jnp.bfloat16).reshape(NX, 4, PIECE, D)
        for g in range(NX):
            for s in range(4):
                out_ref[i, s, g] = done[g, s]

    @pl.loop(1, NZ)
    def _(r):
        leaf_z(r).wait_send()
        pool_to_z(r).wait_send()

    @pl.loop(0, NZ)
    def _(r):
        @pl.loop(1, NS)
        def _(o):
            leaf_s(r, o).wait_send()
            sel_s(r, o).wait_send()

    @pl.loop(1, NS)
    def _(o):
        pool_to_s(o).wait_send()

    @pl.loop(1, NX)
    def _(o):
        weights(o).wait_send()
        qkv_x(o).wait_send()
        resid_x(o).wait_send()
        att_x(o).wait_send()

    for copy in chain_p + chain_m:
        copy.wait_send()


def tables(rotated_slot, selected):
    b = lax.axis_index("balls")
    y = b // (NZ * NC)
    z = (b // NC) % NZ
    c = b % NC
    k8 = jnp.arange(NS, dtype=jnp.int32)
    z8 = jnp.arange(NZ, dtype=jnp.int32)

    def device(kk, zz):
        return ((kk // NC) * NZ + zz) * NC + kk % NC

    def slot(dev):
        return ((dev // (NZ * NC)) * NC + dev % NC) * NZ + (dev // NC) % NZ

    target = lax.dynamic_slice_in_dim(rotated_slot, b * 32, 32) // 32
    dest = device(k8[None, :], z8[:, None]).reshape(64)
    leaf = jnp.arange(32, dtype=jnp.int32)
    send = jnp.sum(jnp.where(dest[:, None] == target[None, :], leaf[None, :], 0), axis=1)
    place = b * 32 + leaf
    every = jnp.arange(rotated_slot.shape[0], dtype=jnp.int32)
    source = jnp.sum(
        jnp.where(place[:, None] == rotated_slot[None, :], every[None, :] // 32, 0), axis=1
    )
    picks = selected.reshape(NY, NZ, NC, 8 * TOPK)
    rows = lax.dynamic_index_in_dim(picks, z, axis=1, keepdims=False).reshape(NS, 8 * TOPK)
    origin = (y * NZ + z8) * NC + c
    chosen = jnp.sum(
        jnp.where(rows[None] // 8 == origin[:, None, None], rows[None] % 8, 0), axis=-1
    )
    mine = lax.dynamic_slice_in_dim(selected, b * 8, 8).reshape(8 * TOPK)
    return jnp.concatenate([send, slot(source), chosen.reshape(64), slot(mine // 8)])


def on_device(
    particles, query_weight, key_weight, value_weight, out_weight, up_weight, down_weight,
    rotated_slot, selected,
):
    pad = jnp.zeros((D, 64), jnp.bfloat16)
    key_value = jnp.concatenate([key_weight, value_weight, pad], axis=1)
    weight = jnp.concatenate([query_weight, key_value], axis=1)
    bf, f32 = jnp.bfloat16, jnp.float32
    vmem = pl.BlockSpec(memory_space=pltpu.VMEM)
    hbm = pl.BlockSpec(memory_space=pl.ANY)
    sem = pltpu.SemaphoreType.DMA
    kv = pltpu.VMEM((8, 2 * HEAD, BALL), bf)
    result = pl.pallas_call(
        kernel,
        name="layer",
        out_shape=jax.ShapeDtypeStruct((2, 4, NX, PIECE, D), bf),
        in_specs=[pl.BlockSpec(memory_space=pltpu.SMEM), vmem, vmem, vmem, hbm, hbm, hbm],
        out_specs=vmem,
        scratch_shapes=[
            pltpu.VMEM((D, D), bf), pltpu.VMEM((D, FF), bf), pltpu.VMEM((FF, D), bf),
            pltpu.VMEM((NX, D, 256), bf),
            pltpu.VMEM((NZ, NS, PIECE, D), bf), pltpu.VMEM((NZ, NS, PIECE, D), bf),
            pltpu.VMEM((NS * NZ, PIECE, D), bf), pltpu.VMEM((32, PIECE, D), bf),
            pltpu.VMEM((NX, 512, 256), bf), pltpu.VMEM((NX, 512, 256), bf),
            pltpu.VMEM((NX, 8, PIECE, D), bf),
            kv, kv, kv, kv, kv, kv, kv, kv,
            pltpu.VMEM((NZ, NS, 2 * HEAD, BALL), bf),
            pltpu.VMEM((NS * NZ, 2 * HEAD, BALL), bf),
            pltpu.VMEM((8, 128), f32), pltpu.VMEM((NZ, 8, 128), f32),
            pltpu.VMEM((NS, NZ, 8, 128), f32),
            pltpu.VMEM((4, 128, 6 * BALL), bf), pltpu.VMEM((4, 256, 6 * BALL), bf),
            pltpu.VMEM((8, BALL, 128), bf), pltpu.VMEM((NX, 2, BALL, 128), bf),
            sem((3,)), sem((NX,)), sem((NX,)), sem((NZ,)), sem((NZ,)),
            sem((NZ, NS)), sem((NZ, NS)), sem((NX,)), sem((NX,)), sem((NX,)), sem((NX,)),
            sem((8,)), sem((8,)), sem((NZ, NS)), sem((NZ, NS)), sem((NZ,)), sem((NZ,)),
            sem((NS,)), sem((NS,)), sem((NX,)), sem((NX,)),
        ],
        compiler_params=pltpu.CompilerParams(
            collective_id=0, has_side_effects=True, vmem_limit_bytes=60 * 1024 * 1024
        ),
    )(
        tables(rotated_slot, selected),
        particles.reshape(128, PIECE, D),
        weight,
        key_value.T,
        out_weight, up_weight, down_weight,
    )
    return result.reshape(512, D)


def solution(mesh):
    in_specs = (
        P("balls", None), P(None, "heads"), P(None, "heads"), P(None, "heads"),
        P(), P(), P(), P(), P(),
    )
    out_specs = P(("balls", "heads"), None)
    return jax.shard_map(
        on_device, mesh=mesh, in_specs=in_specs, out_specs=out_specs, check_vma=False
    )
```

```python
import functools
import math

import jax
import jax.numpy as jnp
from jax import lax
from jax.experimental import pallas as pl
from jax.experimental.pallas import tpu as pltpu
from jax.sharding import PartitionSpec as P

HEAD = 32
BALL = 256
LEAF = 64
TOPK = 3
NX, NY, NZ, NC = 4, 4, 8, 2
NS = NY * NC
PIECE = LEAF // NX
D = 512
FF = 2048
SCALE = math.log2(math.e) / math.sqrt(HEAD)
NT = (((1,), (1,)), ((), ()))
Z_ORDER = (4, 5, 3, 6, 2, 7, 1)


def rms_rows(matrix):
    wide = matrix.astype(jnp.float32)
    return (wide * lax.rsqrt(jnp.mean(wide * wide, axis=-1, keepdims=True) + 1e-05)).astype(
        jnp.bfloat16
    )


def dot32(left, right, dims=None):
    if dims is None:
        return jnp.dot(left, right, preferred_element_type=jnp.float32)
    return lax.dot_general(left, right, dims, preferred_element_type=jnp.float32)


def kernel(
    rs_ref, sel_ref, wq_ref, wk_ref, wv_ref, p_hbm, wo_hbm, up_hbm, down_hbm, out_ref,
    p_ref, wo_ref, up_ref, down_ref, wq_all, wkv_all,
    tab_v, tab_a, tab_b,
    leaf_stage, leaf_mid, leaf_recv, rotq, q_stage, q_recv, kv_stage, kv_recv, rres,
    kv_own, agp1, agp2, agp3, agm1, agm2, agm3, ag4,
    sel_stage, sel_recv, pool_own, pool_z, pool_all,
    kt_a, vt_a, kt_b, vt_b, early, tops, att_st, att_recv,
    load_sem, ws, wr, lzs, lzr, lss, lsr, xs, xr, rs, rr,
    ags, agr, sss, ssr, pzs, pzr, pss, psr, ats, atr,
):
    b = lax.axis_index("balls")
    h = lax.axis_index("heads")
    y = b // (NZ * NC)
    z = (b // NC) % NZ
    c = b % NC
    k = y * NC + c

    def z_peer(r):
        return {"balls": (y * NZ + (z + r) % NZ) * NC + c, "heads": h}

    def s_peer(o):
        kk = (k + o) % NS
        return {"balls": ((kk // NC) * NZ + z) * NC + kk % NC, "heads": h}

    def x_peer(o):
        return {"balls": b, "heads": (h + o) % NX}

    def remote(src, dst, send, recv, peer):
        return pltpu.make_async_remote_copy(
            src_ref=src, dst_ref=dst, send_sem=send, recv_sem=recv,
            device_id=peer, device_id_type=pl.DeviceIdType.MESH,
        )

    barrier = pltpu.get_barrier_semaphore()

    @pl.loop(1, NZ)
    def _(r):
        pl.semaphore_signal(barrier, 1, device_id=z_peer(r))

    @pl.loop(1, NS)
    def _(o):
        pl.semaphore_signal(barrier, 1, device_id=s_peer(o))

    @pl.loop(1, NX)
    def _(o):
        pl.semaphore_signal(barrier, 1, device_id=x_peer(o))

    load_p = pltpu.make_async_copy(p_hbm, p_ref, load_sem.at[0])
    load_p.start()
    loads = [
        pltpu.make_async_copy(wo_hbm, wo_ref, load_sem.at[1]),
        pltpu.make_async_copy(up_hbm, up_ref, load_sem.at[2]),
        pltpu.make_async_copy(down_hbm, down_ref, load_sem.at[3]),
    ]

    def iota(shape, axis):
        return lax.broadcasted_iota(jnp.int32, shape, axis)

    def slot(dev):
        return (((dev >> 4) * NC + (dev & 1)) << 3) + ((dev >> 1) & 7)

    def device(kk, zz):
        return (((kk >> 1) << 3) + zz) * NC + (kk & 1)

    def table(parts, at, target, which):
        used = sum(part.shape[0] for part in parts)
        if used < 128:
            parts = parts + [jnp.zeros((128 - used, 128), jnp.int32)]
        square = jnp.concatenate(parts, axis=0)
        tab_v[pl.ds(8 * at, 8)] = jnp.broadcast_to(
            jnp.max(square.T, axis=0, keepdims=True) & 63, (8, 128)
        )
        copy = pltpu.make_async_copy(tab_v.at[pl.ds(8 * at, 8)], target, load_sem.at[which])
        copy.start()
        return copy

    i64, lane64 = iota((64, 128), 0), iota((64, 128), 1)
    own_row = rs_ref[pl.ds(b // 4, 1), :]
    found = ((own_row >> 5) == device(i64 & 7, i64 >> 3)) & ((lane64 >> 5) == b % 4)
    send = jnp.where(found, lane64 & 31, 0)
    table_a = table([send], 0, tab_a, 4)

    def selected_tables():
        place, lane = iota((32, 128), 0) + b * 32, iota((32, 128), 1)
        take = jnp.zeros((32, 128), jnp.int32)
        for row in range(16):
            found = rs_ref[pl.ds(row, 1), :] == place
            take = jnp.maximum(take, jnp.where(found, slot(row * 4 + (lane >> 5)), 0))
        i, ball = iota((64, 512), 0), iota((64, 512), 1)
        reader = (ball >> 3) == device(i & 7, z)
        origin = (y * NZ + (i >> 3)) * NC + c
        e, ball_e = iota((32, 512), 0), iota((32, 512), 1)
        give = jnp.zeros((64, 512), jnp.int32)
        fetch = jnp.zeros((32, 512), jnp.int32)
        for t in range(TOPK):
            pick = sel_ref[pl.ds(t, 1), :]
            give = jnp.maximum(give, jnp.where(reader & ((pick >> 3) == origin), pick & 7, 0))
            mine = (ball_e - b * 8) * TOPK + t == e
            fetch = jnp.maximum(fetch, jnp.where(mine, slot(pick >> 3), 0))
        give = functools.reduce(jnp.maximum, [give[:, 128 * q : 128 * q + 128] for q in range(4)])
        fetch = functools.reduce(jnp.maximum, [fetch[:, 128 * q : 128 * q + 128] for q in range(4)])
        return table([give, take, fetch], 1, tab_b, 5)

    table_b = selected_tables()
    wq_all[h] = wq_ref[...]
    wkv_all[h, pl.ds(0, HEAD)] = wk_ref[...]
    wkv_all[h, pl.ds(HEAD, HEAD)] = wv_ref[...]

    load_p.wait()
    table_a.wait()

    @pl.loop(0, NZ)
    def _(zd):
        for kk in range(NS):
            leaf_stage[zd, kk] = p_ref[tab_a[0, zd * NS + kk] * NX + h]

    leaf_mid[z] = leaf_stage[z]
    for load in loads:
        load.start()
    pl.semaphore_wait(barrier, (NZ - 1) + (NS - 1) + (NX - 1))

    def leaf_z(r):
        return remote(
            leaf_stage.at[(z + r) % NZ], leaf_mid.at[z], lzs.at[r], lzr.at[r], z_peer(r)
        )

    for r in Z_ORDER:
        leaf_z(r).start()

    def weights(o, part):
        full = (wq_all, wkv_all)[part]
        return remote(full.at[h], full.at[h], ws.at[part, o], wr.at[part, o], x_peer(o))

    @pl.loop(1, NX)
    def _(o):
        weights(o, 0).start()
        weights(o, 1).start()

    ones8 = jnp.ones((8, BALL), jnp.bfloat16)
    row8 = iota((8, 2 * HEAD), 0)

    def own_ball(i, pooled):
        rows = p_ref[pl.ds(i * 16, 16)].reshape(BALL, D)
        kvt = dot32(wkv_all[h], rms_rows(rows), NT).astype(jnp.bfloat16)
        kv_own[i] = kvt
        total = dot32(ones8, kvt, NT) * (1.0 / math.sqrt(BALL))
        return jnp.where(row8 == i, total.astype(jnp.bfloat16).astype(jnp.float32), pooled)

    pooled = lax.fori_loop(0, 8, own_ball, jnp.zeros((8, 2 * HEAD), jnp.float32))
    pool_own[...] = jnp.concatenate([pooled, jnp.zeros((8, 2 * HEAD), jnp.float32)], axis=1)

    def pool_to_z(r):
        return remote(pool_own, pool_z.at[z], pzs.at[r], pzr.at[r], z_peer(r))

    @pl.loop(1, NZ)
    def _(r):
        pool_to_z(r).start()

    rings = ((kv_own, agp1, agp2, agp3, ag4), (kv_own, agm1, agm2, agm3, ag4))

    def hop(way, step, part):
        at = pl.ds(4 * part, 4)
        return remote(
            rings[way][step].at[at], rings[way][step + 1].at[at],
            ags.at[way, step, part], agr.at[way, step, part], z_peer(1 if way == 0 else NZ - 1),
        )

    def relay(step, part):
        for way in range(2):
            hop(way, step - 1, part).wait_recv()
            if step < 3 or part == way:
                hop(way, step, part).start()

    for part in range(2):
        hop(0, 0, part).start()
        hop(1, 0, part).start()

    pool_z[z] = pool_own[...]

    for kt, vt in ((kt_a, vt_a), (kt_b, vt_b)):
        kt[...] = jnp.zeros_like(kt)
        vt[...] = jnp.zeros_like(vt)
        for j in range(4):
            vt[j, pl.ds(128 + HEAD * j, HEAD), :] = jnp.ones((HEAD, 3 * BALL), jnp.bfloat16)

    def place(kt, vt, block, kvt):
        width = kvt.shape[1]
        for j in range(4):
            kt[j, pl.ds(HEAD * j, HEAD), pl.ds(block * BALL, width)] = kvt[:HEAD]
            vt[j, pl.ds(HEAD * j, HEAD), pl.ds(block * BALL, width)] = kvt[HEAD:]

    def leaf_s(r, o):
        zs = (z + NZ - r) % NZ
        kk = (k + o) % NS
        return remote(
            leaf_mid.at[zs, kk], leaf_recv.at[k * NZ + zs], lss.at[r, o], lsr.at[r, o], s_peer(o)
        )

    for r in (0,) + Z_ORDER:
        if r > 0:
            leaf_z(r).wait_recv()

        @pl.loop(1, NS)
        def _(o):
            leaf_s(r, o).start()

        zs = (z + NZ - r) % NZ
        leaf_recv[k * NZ + zs] = leaf_mid[zs, k]

    def pool_to_s(o):
        return remote(pool_z, pool_all.at[k], pss.at[o], psr.at[o], s_peer(o))

    @pl.loop(1, NZ)
    def _(r):
        pool_to_z(r).wait_recv()

    @pl.loop(1, NS)
    def _(o):
        pool_to_s(o).start()

    pool_all[k] = pool_z[...]

    table_b.wait()

    def sel_s(r, o):
        zs = (z + NZ - r) % NZ
        kk = (k + o) % NS
        return remote(
            sel_stage.at[r, kk], sel_recv.at[k * NZ + zs], sss.at[r, o], ssr.at[r, o], s_peer(o)
        )

    def forward(source, r):
        zs = (z + NZ - r) % NZ

        @pl.loop(0, NS)
        def _(kk):
            sel_stage[r, kk] = source[tab_b[0, zs * NS + kk]]

        sel_recv[k * NZ + zs] = sel_stage[r, k]

        @pl.loop(1, NS)
        def _(o):
            sel_s(r, o).start()

    forward(kv_own, 0)
    relay(1, 0)

    @pl.loop(1, NX)
    def _(o):
        weights(o, 0).wait_recv()
        weights(o, 1).wait_recv()

    @pl.loop(0, NZ)
    def _(r):
        @pl.loop(1, NS)
        def _(o):
            leaf_s(r, o).wait_recv()

    @pl.loop(0, 4)
    def _(q):
        for s in range(8):
            rotq[q * 8 + s] = leaf_recv[tab_b[0, 64 + q * 8 + s]]
        rows = rms_rows(rotq[pl.ds(q * 8, 8)].reshape(128, D))
        at = pl.ds(pl.multiple_of(q * 128, 128), 128)
        for g in range(NX):
            q_stage[g, at] = dot32(rows, wq_all[g]).astype(jnp.bfloat16)
            kv_stage[g, :, at] = dot32(wkv_all[g], rows, NT).astype(jnp.bfloat16)

    def resid_x(o):
        return remote(
            rotq.at[pl.ds(((h + o) % NX) * 8, 8)], rres.at[h], rs.at[o], rr.at[o], x_peer(o)
        )

    def qkv_x(o, part):
        src, dst = ((q_stage, q_recv), (kv_stage, kv_recv))[part]
        return remote(
            src.at[(h + o) % NX], dst.at[h], xs.at[part, o], xr.at[part, o], x_peer(o)
        )

    for o in (2, 1, 3):
        qkv_x(o, 0).start()
        qkv_x(o, 1).start()

    @pl.loop(1, NX)
    def _(o):
        resid_x(o).start()

    q_recv[h] = q_stage[h]
    kv_recv[h] = kv_stage[h]
    rres[h] = rotq[pl.ds(h * 8, 8)]

    relay(1, 1)
    forward(agp1, 1)
    forward(agm1, 7)
    relay(2, 0)
    relay(2, 1)
    forward(agp2, 2)
    forward(agm2, 6)

    eye = (iota((2 * HEAD, 128), 0) == iota((2 * HEAD, 128), 1)).astype(jnp.bfloat16)

    @pl.loop(1, NS)
    def _(o):
        pool_to_s(o).wait_recv()

    pool_rows = pool_all[...].reshape(2 * BALL, 128).astype(jnp.bfloat16)
    place(kt_a, vt_a, 1, dot32(eye, pool_rows, NT).astype(jnp.bfloat16))

    @pl.loop(1, NX)
    def _(o):
        qkv_x(o, 0).wait_recv()
        qkv_x(o, 1).wait_recv()

    lane_head = iota((BALL, 128), 1) // HEAD
    left = iota((2 * HEAD, 128), 1) < 64

    def query_rows(ball):
        at = pl.ds(pl.multiple_of(ball * 64, 64), 64)
        return jnp.concatenate([q_recv[g, at] for g in range(NX)], axis=0)

    def attend_own(pair, i):
        ball = pair * 2 + i
        at = pl.ds(pl.multiple_of(pair * 128, 128), 128)
        tiles = [kv_recv[g, :, at] for g in range(NX)]
        rolled = [pltpu.roll(tile.astype(jnp.float32), 64, 1).astype(jnp.bfloat16) for tile in tiles]
        if i == 0:
            halves = [jnp.where(left, tiles[g], rolled[g + 1]) for g in (0, 2)]
        else:
            halves = [jnp.where(left, rolled[g], tiles[g + 1]) for g in (0, 2)]
        place(kt_a, vt_a, 0, jnp.concatenate(halves, axis=1))
        q = query_rows(ball)
        total = jnp.zeros((BALL, 256), jnp.float32)
        top_all = jnp.zeros((BALL, 128), jnp.float32)
        for j in range(4):
            score = dot32(q, kt_a[j])
            top = jnp.max(score, axis=-1, keepdims=True)
            weight = jnp.exp2((score - top) * SCALE).astype(jnp.bfloat16)
            total = total + dot32(weight, vt_a[j], NT)
            top_all = jnp.where(lane_head == j, top, top_all)
        early[ball] = total
        tops[ball] = top_all

    def attend_selected(pair, i):
        ball = pair * 2 + i
        for t in range(TOPK):
            place(kt_b, vt_b, t, sel_recv[tab_b[0, 96 + ball * TOPK + t]])
        q = query_rows(ball)
        total = jnp.zeros((BALL, 256), jnp.float32)
        before = tops[ball]
        after = before
        for j in range(4):
            score = dot32(q, kt_b[j])
            top = jnp.maximum(
                jnp.max(score, axis=-1, keepdims=True), before[:, HEAD * j : HEAD * j + 1]
            )
            weight = jnp.exp2((score - top) * SCALE).astype(jnp.bfloat16)
            total = total + dot32(weight, vt_b[j], NT)
            after = jnp.where(lane_head == j, top, after)
        scale = jnp.exp2((before - after) * SCALE)
        value = total[:, :128] + early[ball, :, :128] * scale
        count = total[:, 128:] + early[ball, :, 128:] * scale
        att_st[ball] = (value / count).astype(jnp.bfloat16)

    def own_pairs(first, last):
        @pl.loop(first, last)
        def _(pair):
            attend_own(pair, 0)
            attend_own(pair, 1)

    own_pairs(0, 2)
    relay(3, 0)
    relay(3, 1)
    forward(agp3, 3)
    forward(agm3, 5)
    own_pairs(2, 4)
    hop(0, 3, 0).wait_recv()
    hop(1, 3, 1).wait_recv()
    forward(ag4, 4)

    @pl.loop(0, NZ)
    def _(r):
        @pl.loop(1, NS)
        def _(o):
            sel_s(r, o).wait_recv()

    def att_x(o):
        return remote(
            att_st.at[pl.ds(((h + o) % NX) * 2, 2)], att_recv.at[h], ats.at[o], atr.at[o], x_peer(o)
        )

    @pl.loop(1, NX + 1)
    def _(o):
        pair = (h + o) % NX
        attend_selected(pair, 0)
        attend_selected(pair, 1)

        @pl.when(o < NX)
        def _():
            att_x(o).start()

    att_recv[h] = att_st[pl.ds(h * 2, 2)]

    for load in loads:
        load.wait()

    @pl.loop(1, NX)
    def _(o):
        resid_x(o).wait_recv()

    @pl.loop(1, NX)
    def _(o):
        att_x(o).wait_recv()
    @pl.loop(0, 2)
    def _(i):
        heads = jnp.concatenate([att_recv[g, i] for g in range(NX)], axis=1)
        base = jnp.concatenate(
            [rres[g, pl.ds(i * 4, 4)].reshape(64, D) for g in range(NX)], axis=0
        )
        resid = (base.astype(jnp.float32) + dot32(heads, wo_ref[...])).astype(jnp.bfloat16)
        mlp_in = rms_rows(resid)

        def hidden(f, total):
            cols = pl.ds(pl.multiple_of(f * 512, 512), 512)
            inner = jax.nn.gelu(dot32(mlp_in, up_ref[:, cols])).astype(jnp.bfloat16)
            return total + dot32(inner, down_ref[cols, :])

        done = lax.fori_loop(0, FF // 512, hidden, resid.astype(jnp.float32))
        done = done.astype(jnp.bfloat16).reshape(NX, 4, PIECE, D)
        for g in range(NX):
            for s in range(4):
                out_ref[i, s, g] = done[g, s]

    @pl.loop(1, NZ)
    def _(r):
        leaf_z(r).wait_send()
        pool_to_z(r).wait_send()

    @pl.loop(0, NZ)
    def _(r):
        @pl.loop(1, NS)
        def _(o):
            leaf_s(r, o).wait_send()
            sel_s(r, o).wait_send()

    @pl.loop(1, NS)
    def _(o):
        pool_to_s(o).wait_send()

    @pl.loop(1, NX)
    def _(o):
        for part in range(2):
            weights(o, part).wait_send()
            qkv_x(o, part).wait_send()
        resid_x(o).wait_send()
        att_x(o).wait_send()

    for way in range(2):
        for step in range(4):
            for part in range(2):
                if step < 3 or part == way:
                    hop(way, step, part).wait_send()


def on_device(
    particles, query_weight, key_weight, value_weight, out_weight, up_weight, down_weight,
    rotated_slot, selected,
):
    bf, f32 = jnp.bfloat16, jnp.float32
    vmem = pl.BlockSpec(memory_space=pltpu.VMEM)
    hbm = pl.BlockSpec(memory_space=pl.ANY)
    sem = pltpu.SemaphoreType.DMA
    kv = pltpu.VMEM((8, 2 * HEAD, BALL), bf)
    result = pl.pallas_call(
        kernel,
        name="layer",
        out_shape=jax.ShapeDtypeStruct((2, 4, NX, PIECE, D), bf),
        in_specs=[vmem] * 5 + [hbm] * 4,
        out_specs=vmem,
        scratch_shapes=[
            pltpu.VMEM((128, PIECE, D), bf),
            pltpu.VMEM((D, D), bf), pltpu.VMEM((D, FF), bf), pltpu.VMEM((FF, D), bf),
            pltpu.VMEM((NX, D, 128), bf), pltpu.VMEM((NX, 2 * HEAD, D), bf),
            pltpu.VMEM((16, 128), jnp.int32),
            pltpu.SMEM((8, 128), jnp.int32), pltpu.SMEM((8, 128), jnp.int32),
            pltpu.VMEM((NZ, NS, PIECE, D), bf), pltpu.VMEM((NZ, NS, PIECE, D), bf),
            pltpu.VMEM((NS * NZ, PIECE, D), bf), pltpu.VMEM((32, PIECE, D), bf),
            pltpu.VMEM((NX, 512, 128), bf), pltpu.VMEM((NX, 512, 128), bf),
            pltpu.VMEM((NX, 2 * HEAD, 512), bf), pltpu.VMEM((NX, 2 * HEAD, 512), bf),
            pltpu.VMEM((NX, 8, PIECE, D), bf),
            kv, kv, kv, kv, kv, kv, kv, kv,
            pltpu.VMEM((NZ, NS, 2 * HEAD, BALL), bf),
            pltpu.VMEM((NS * NZ, 2 * HEAD, BALL), bf),
            pltpu.VMEM((8, 128), f32), pltpu.VMEM((NZ, 8, 128), f32),
            pltpu.VMEM((NS, NZ, 8, 128), f32),
            pltpu.VMEM((4, 128, 3 * BALL), bf), pltpu.VMEM((4, 256, 3 * BALL), bf),
            pltpu.VMEM((4, 128, 3 * BALL), bf), pltpu.VMEM((4, 256, 3 * BALL), bf),
            pltpu.VMEM((8, BALL, 256), f32), pltpu.VMEM((8, BALL, 128), f32),
            pltpu.VMEM((8, BALL, 128), bf), pltpu.VMEM((NX, 2, BALL, 128), bf),
            sem((6,)), sem((2, NX)), sem((2, NX)), sem((NZ,)), sem((NZ,)),
            sem((NZ, NS)), sem((NZ, NS)), sem((2, NX)), sem((2, NX)), sem((NX,)), sem((NX,)),
            sem((2, 4, 2)), sem((2, 4, 2)), sem((NZ, NS)), sem((NZ, NS)), sem((NZ,)), sem((NZ,)),
            sem((NS,)), sem((NS,)), sem((NX,)), sem((NX,)),
        ],
        compiler_params=pltpu.CompilerParams(
            collective_id=0, has_side_effects=True, vmem_limit_bytes=60 * 1024 * 1024
        ),
    )(
        rotated_slot.reshape(16, 128), selected.T, query_weight, key_weight.T, value_weight.T,
        particles.reshape(128, PIECE, D), out_weight, up_weight, down_weight,
    )
    return result.reshape(512, D)


def solution(mesh):
    in_specs = (
        P("balls", None), P(None, "heads"), P(None, "heads"), P(None, "heads"),
        P(), P(), P(), P(), P(),
    )
    out_specs = P(("balls", "heads"), None)
    return jax.shard_map(
        on_device, mesh=mesh, in_specs=in_specs, out_specs=out_specs, check_vma=False
    )
```

```python
import functools
import math

import jax
import jax.numpy as jnp
from jax import lax
from jax.experimental import pallas as pl
from jax.experimental.pallas import tpu as pltpu
from jax.sharding import PartitionSpec as P

HEAD = 32
BALL = 256
LEAF = 64
TOPK = 3
NX, NY, NZ, NC = 4, 4, 8, 2
NS = NY * NC
PIECE = LEAF // NX
D = 512
FF = 2048
SCALE = math.log2(math.e) / math.sqrt(HEAD)
NT = (((1,), (1,)), ((), ()))
Z_ORDER = (4, 5, 3, 6, 2, 7, 1)


def rms_rows(matrix):
    wide = matrix.astype(jnp.float32)
    return (wide * lax.rsqrt(jnp.mean(wide * wide, axis=-1, keepdims=True) + 1e-05)).astype(
        jnp.bfloat16
    )


def dot32(left, right, dims=None):
    if dims is None:
        return jnp.dot(left, right, preferred_element_type=jnp.float32)
    return lax.dot_general(left, right, dims, preferred_element_type=jnp.float32)


def kernel(
    rs_hbm, sel_hbm, wq_hbm, wk_hbm, wv_hbm, p_hbm, wo_hbm, up_hbm, down_hbm, out_ref,
    rs_ref, sel_ref, wq_ref, p_ref, wo_ref, up_ref, down_ref, w_all,
    tab_v, tab_a, tab_b,
    leaf_stage, leaf_mid, leaf_recv, rotq, q_stage, q_recv, rres,
    kv_own, agp1, agp2, agp3, agm1, agm2, agm3, ag4,
    sel_stage, sel_recv, pool_own, pool_z, pool_all,
    k_a, vt_a, k_b, vt_b, values, counts, tops, queries, score_buf, att_st, att_recv,
    load_sem, ws, wr, lzs, lzr, lss, lsr, xs, xr, rs, rr,
    ags, agr, sss, ssr, pzs, pzr, pss, psr, ats, atr,
):
    b = lax.axis_index("balls")
    h = lax.axis_index("heads")
    y = b // (NZ * NC)
    z = (b // NC) % NZ
    c = b % NC
    k = y * NC + c

    def z_peer(r):
        return {"balls": (y * NZ + (z + r) % NZ) * NC + c, "heads": h}

    def s_peer(o):
        kk = (k + o) % NS
        return {"balls": ((kk // NC) * NZ + z) * NC + kk % NC, "heads": h}

    def x_peer(o):
        return {"balls": b, "heads": (h + o) % NX}

    def remote(src, dst, send, recv, peer):
        return pltpu.make_async_remote_copy(
            src_ref=src, dst_ref=dst, send_sem=send, recv_sem=recv,
            device_id=peer, device_id_type=pl.DeviceIdType.MESH,
        )

    barrier = pltpu.get_barrier_semaphore()

    @pl.loop(1, NZ)
    def _(r):
        pl.semaphore_signal(barrier, 1, device_id=z_peer(r))

    @pl.loop(1, NS)
    def _(o):
        pl.semaphore_signal(barrier, 1, device_id=s_peer(o))

    @pl.loop(1, NX)
    def _(o):
        pl.semaphore_signal(barrier, 1, device_id=x_peer(o))

    small = [
        pltpu.make_async_copy(rs_hbm, rs_ref, load_sem.at[6]),
        pltpu.make_async_copy(sel_hbm, sel_ref, load_sem.at[7]),
        pltpu.make_async_copy(wq_hbm, wq_ref, load_sem.at[8]),
        pltpu.make_async_copy(wk_hbm, w_all.at[h, pl.ds(128, HEAD)], load_sem.at[9]),
        pltpu.make_async_copy(wv_hbm, w_all.at[h, pl.ds(160, HEAD)], load_sem.at[10]),
    ]
    load_p = pltpu.make_async_copy(p_hbm, p_ref, load_sem.at[0])
    small[0].start()
    load_p.start()
    for load in small[1:]:
        load.start()
    loads = [
        pltpu.make_async_copy(wo_hbm, wo_ref, load_sem.at[1]),
        pltpu.make_async_copy(up_hbm, up_ref, load_sem.at[2]),
        pltpu.make_async_copy(down_hbm, down_ref, load_sem.at[3]),
    ]

    def iota(shape, axis):
        return lax.broadcasted_iota(jnp.int32, shape, axis)

    def slot(dev):
        return (((dev >> 4) * NC + (dev & 1)) << 3) + ((dev >> 1) & 7)

    def device(kk, zz):
        return (((kk >> 1) << 3) + zz) * NC + (kk & 1)

    def table(parts, at, target, which):
        used = sum(part.shape[0] for part in parts)
        if used < 128:
            parts = parts + [jnp.zeros((128 - used, 128), jnp.int32)]
        square = jnp.concatenate(parts, axis=0)
        tab_v[pl.ds(8 * at, 8)] = jnp.broadcast_to(
            jnp.max(square.T, axis=0, keepdims=True) & 63, (8, 128)
        )
        copy = pltpu.make_async_copy(tab_v.at[pl.ds(8 * at, 8)], target, load_sem.at[which])
        copy.start()
        return copy

    i64, lane64 = iota((64, 128), 0), iota((64, 128), 1)
    small[0].wait()
    own_row = rs_ref[pl.ds(b // 4, 1), :]
    found = ((own_row >> 5) == device(i64 & 7, i64 >> 3)) & ((lane64 >> 5) == b % 4)
    send = jnp.where(found, lane64 & 31, 0)
    table_a = table([send], 0, tab_a, 4)

    def selected_tables():
        place, lane = iota((32, 128), 0) + b * 32, iota((32, 128), 1)
        take = jnp.zeros((32, 128), jnp.int32)
        for row in range(16):
            found = rs_ref[pl.ds(row, 1), :] == place
            take = jnp.maximum(take, jnp.where(found, slot(row * 4 + (lane >> 5)), 0))
        i, ball = iota((64, 512), 0), iota((64, 512), 1)
        reader = (ball >> 3) == device(i & 7, z)
        origin = (y * NZ + (i >> 3)) * NC + c
        e, ball_e = iota((32, 512), 0), iota((32, 512), 1)
        give = jnp.zeros((64, 512), jnp.int32)
        fetch = jnp.zeros((32, 512), jnp.int32)
        for t in range(TOPK):
            pick = sel_ref[pl.ds(t, 1), :]
            give = jnp.maximum(give, jnp.where(reader & ((pick >> 3) == origin), pick & 7, 0))
            mine = (ball_e - b * 8) * TOPK + t == e
            fetch = jnp.maximum(fetch, jnp.where(mine, slot(pick >> 3), 0))
        give = functools.reduce(jnp.maximum, [give[:, 128 * q : 128 * q + 128] for q in range(4)])
        fetch = functools.reduce(jnp.maximum, [fetch[:, 128 * q : 128 * q + 128] for q in range(4)])
        return table([give, take, fetch], 1, tab_b, 5)

    load_p.wait()
    table_a.wait()

    @pl.loop(0, NZ)
    def _(zd):
        for kk in range(NS):
            leaf_stage[zd, kk] = p_ref[tab_a[0, zd * NS + kk] * NX + h]

    leaf_mid[z] = leaf_stage[z]
    for load in loads:
        load.start()
    for load in small[1:]:
        load.wait()
    w_all[h, pl.ds(0, 128)] = wq_ref[...].astype(jnp.float32).T.astype(jnp.bfloat16)
    table_b = selected_tables()
    pl.semaphore_wait(barrier, (NZ - 1) + (NS - 1) + (NX - 1))

    def leaf_z(r):
        return remote(
            leaf_stage.at[(z + r) % NZ], leaf_mid.at[z], lzs.at[r], lzr.at[r], z_peer(r)
        )

    for r in Z_ORDER:
        leaf_z(r).start()

    def weights(o):
        return remote(w_all.at[h], w_all.at[h], ws.at[o], wr.at[o], x_peer(o))

    @pl.loop(1, NX)
    def _(o):
        weights(o).start()

    ones8 = jnp.ones((8, BALL), jnp.bfloat16)
    row8 = iota((8, 2 * HEAD), 0)

    def own_ball(i, pooled):
        rows = p_ref[pl.ds(i * 16, 16)].reshape(BALL, D)
        kvt = dot32(w_all[h, pl.ds(128, 2 * HEAD)], rms_rows(rows), NT).astype(jnp.bfloat16)
        kv_own[i] = kvt
        total = dot32(ones8, kvt, NT) * (1.0 / math.sqrt(BALL))
        return jnp.where(row8 == i, total.astype(jnp.bfloat16).astype(jnp.float32), pooled)

    pooled = lax.fori_loop(0, 8, own_ball, jnp.zeros((8, 2 * HEAD), jnp.float32))
    pool_own[...] = jnp.concatenate([pooled, jnp.zeros((8, 2 * HEAD), jnp.float32)], axis=1)

    def pool_to_z(r):
        return remote(pool_own, pool_z.at[z], pzs.at[r], pzr.at[r], z_peer(r))

    @pl.loop(1, NZ)
    def _(r):
        pool_to_z(r).start()

    rings = ((kv_own, agp1, agp2, agp3, ag4), (kv_own, agm1, agm2, agm3, ag4))

    def hop(way, step, part):
        at = pl.ds(4 * part, 4)
        return remote(
            rings[way][step].at[at], rings[way][step + 1].at[at],
            ags.at[way, step, part], agr.at[way, step, part], z_peer(1 if way == 0 else NZ - 1),
        )

    def relay(step, part):
        for way in range(2):
            hop(way, step - 1, part).wait_recv()
            if step < 3 or part == way:
                hop(way, step, part).start()

    for part in range(2):
        hop(0, 0, part).start()
        hop(1, 0, part).start()

    pool_z[z] = pool_own[...]

    table_b.wait()

    def sel_s(r, o):
        zs = (z + NZ - r) % NZ
        kk = (k + o) % NS
        return remote(
            sel_stage.at[r, kk], sel_recv.at[k * NZ + zs], sss.at[r, o], ssr.at[r, o], s_peer(o)
        )

    def forward(source, r):
        zs = (z + NZ - r) % NZ

        @pl.loop(0, NS)
        def _(kk):
            sel_stage[r, kk] = source[tab_b[0, zs * NS + kk]]

        sel_recv[k * NZ + zs] = sel_stage[r, k]

        @pl.loop(1, NS)
        def _(o):
            sel_s(r, o).start()

    forward(kv_own, 0)

    for vt in (vt_a, vt_b):
        for i in range(2):
            vt[i, pl.ds(HEAD, HEAD), :] = jnp.ones((HEAD, 3 * BALL), jnp.bfloat16)

    def place(keys, vt, i, block, kvt):
        at = pl.ds(block * BALL, kvt.shape[1])
        keys[i, at, :] = kvt[:HEAD].astype(jnp.float32).T.astype(jnp.bfloat16)
        vt[i, pl.ds(0, HEAD), at] = kvt[HEAD:].astype(jnp.bfloat16)

    def leaf_s(r, o):
        zs = (z + NZ - r) % NZ
        kk = (k + o) % NS
        return remote(
            leaf_mid.at[zs, kk], leaf_recv.at[k * NZ + zs], lss.at[r, o], lsr.at[r, o], s_peer(o)
        )

    for r in (0,) + Z_ORDER:
        if r > 0:
            leaf_z(r).wait_recv()

        @pl.loop(1, NS)
        def _(o):
            leaf_s(r, o).start()

        zs = (z + NZ - r) % NZ
        leaf_recv[k * NZ + zs] = leaf_mid[zs, k]

    relay(1, 0)

    def pool_to_s(o):
        return remote(pool_z, pool_all.at[k], pss.at[o], psr.at[o], s_peer(o))

    @pl.loop(1, NZ)
    def _(r):
        pool_to_z(r).wait_recv()

    @pl.loop(1, NS)
    def _(o):
        pool_to_s(o).start()

    pool_all[k] = pool_z[...]


    relay(1, 1)
    forward(agp1, 1)
    forward(agm1, 7)

    @pl.loop(1, NX)
    def _(o):
        weights(o).wait_recv()

    @pl.loop(0, NZ)
    def _(r):
        @pl.loop(1, NS)
        def _(o):
            leaf_s(r, o).wait_recv()


    def qkv_x(o, q):
        return remote(
            q_stage.at[(h + o) % NX, q], q_recv.at[h, q], xs.at[o, q], xr.at[o, q], x_peer(o)
        )

    def project(q):
        for s in range(8):
            rotq[q * 8 + s] = leaf_recv[tab_b[0, 64 + q * 8 + s]]
        rows = rms_rows(rotq[pl.ds(q * 8, 8)].reshape(128, D))
        for g in range(NX):
            q_stage[g, q] = dot32(w_all[g], rows, NT).astype(jnp.bfloat16)
        for o in (2, 1, 3):
            qkv_x(o, q).start()
        q_recv[h, q] = q_stage[h, q]

    def project_two(first):
        @pl.loop(first, first + 2)
        def _(q):
            project(q)

    project_two(0)
    relay(2, 0)
    project_two(2)
    relay(2, 1)
    forward(agp2, 2)
    forward(agm2, 6)

    def resid_x(o):
        return remote(
            rotq.at[pl.ds(((h + o) % NX) * 8, 8)], rres.at[h], rs.at[o], rr.at[o], x_peer(o)
        )

    rres[h] = rotq[pl.ds(h * 8, 8)]
    eye = (iota((2 * HEAD, 128), 0) == iota((2 * HEAD, 128), 1)).astype(jnp.bfloat16)

    @pl.loop(1, NS)
    def _(o):
        pool_to_s(o).wait_recv()

    pool_rows = pool_all[...].reshape(2 * BALL, 128).astype(jnp.bfloat16)
    pool_t = dot32(eye, pool_rows, NT)
    for i in range(2):
        place(k_a, vt_a, i, 1, pool_t)

    left = iota((128 + 2 * HEAD, 128), 1) < 64

    def transposed_rows(pair, i):
        tiles = [q_recv[g, pair] for g in range(NX)]
        rolled = [pltpu.roll(tile.astype(jnp.float32), 64, 1).astype(jnp.bfloat16) for tile in tiles]
        if i == 0:
            halves = [jnp.where(left, tiles[g], rolled[g + 1]) for g in (0, 2)]
        else:
            halves = [jnp.where(left, rolled[g], tiles[g + 1]) for g in (0, 2)]
        return jnp.concatenate(halves, axis=1)

    def run_heads(keys, vt, query, start, finish):
        blocks = [pl.ds(BALL * t, BALL) for t in range(3)]

        def scores(u, t, top):
            score = dot32(keys[u // 4, blocks[t], :], query(u))
            score_buf[u % 2, blocks[t], :] = score
            part = jnp.max(score.reshape(32, 8, BALL), axis=0)
            return part if top is None else jnp.maximum(top, part)

        upcoming = None
        for t in range(3):
            upcoming = scores(0, t, upcoming)
        for u in range(8):
            top = jnp.max(upcoming, axis=0, keepdims=True)
            before = start(u)
            if before is not None:
                top = jnp.maximum(top, before)
            upcoming, result = None, None
            for t in range(3):
                if u < 7:
                    upcoming = scores(u + 1, t, upcoming)
                weight = jnp.exp2((score_buf[u % 2, blocks[t], :] - top) * SCALE)
                part = dot32(vt[u // 4, :, blocks[t]], weight.astype(jnp.bfloat16))
                result = part if result is None else result + part
            finish(u, result[:HEAD], result[HEAD:], top, before)

    def attend_own(pair):
        for i in range(2):
            rows = transposed_rows(pair, i)
            queries[pair * 2 + i] = rows[:128]
            place(k_a, vt_a, i, 0, rows[128:])

        def query(u):
            return queries[pair * 2 + u // 4, pl.ds(HEAD * (u % 4), HEAD)]

        def finish(u, value, count, top, before):
            ball, j = pair * 2 + u // 4, u % 4
            values[ball, pl.ds(HEAD * j, HEAD)] = value
            counts[ball, pl.ds(HEAD * j, HEAD)] = count
            tops[ball, pl.ds(j, 1)] = top

        run_heads(k_a, vt_a, query, lambda u: None, finish)

    def attend_selected(pair, ready):
        for i in range(2):
            for t in range(TOPK):
                place(k_b, vt_b, i, t, sel_recv[tab_b[0, 96 + (pair * 2 + i) * TOPK + t]])

        def query(u):
            return queries[pair * 2 + u // 4, pl.ds(HEAD * (u % 4), HEAD)]

        def start(u):
            return tops[pair * 2 + u // 4, pl.ds(u % 4, 1)]

        parts = []

        def finish(u, value, count, top, before):
            ball, at = pair * 2 + u // 4, pl.ds(HEAD * (u % 4), HEAD)
            scale = jnp.exp2((before - top) * SCALE)
            parts.append((value + values[ball, at] * scale) / (count + counts[ball, at] * scale))
            if u % 4 == 3:
                att_st[ball] = jnp.concatenate(parts[u - 3 :], axis=0).T.astype(jnp.bfloat16)
                ready(u // 4)

        run_heads(k_b, vt_b, query, start, finish)

    def own_pair(pair):
        @pl.loop(1, NX)
        def _(o):
            qkv_x(o, pair).wait_recv()

        attend_own(pair)

    @pl.loop(0, NX)
    def _(pair):
        own_pair(pair)

        @pl.when(pair == 0)
        def _():
            relay(3, 0)

        @pl.when(pair == 1)
        def _():
            relay(3, 1)
            forward(agp3, 3)
            forward(agm3, 5)

        @pl.when(pair == 2)
        def _():
            hop(0, 3, 0).wait_recv()
            hop(1, 3, 1).wait_recv()
            forward(ag4, 4)

            @pl.loop(1, NX)
            def _(o):
                resid_x(o).start()

    @pl.loop(0, NZ)
    def _(r):
        @pl.loop(1, NS)
        def _(o):
            sel_s(r, o).wait_recv()

    def att_x(o, i):
        return remote(
            att_st.at[((h + o) % NX) * 2 + i], att_recv.at[h, i], ats.at[o, i], atr.at[o, i],
            x_peer(o),
        )

    @pl.loop(1, NX)
    def _(o):
        attend_selected((h + o) % NX, lambda i: att_x(o, i).start())

    attend_selected(h, lambda i: None)
    att_recv[h] = att_st[pl.ds(h * 2, 2)]

    for load in loads:
        load.wait()

    @pl.loop(1, NX)
    def _(o):
        resid_x(o).wait_recv()

    @pl.loop(1, NX)
    def _(o):
        att_x(o, 0).wait_recv()
        att_x(o, 1).wait_recv()
    both = [(i, g) for i in range(2) for g in range(NX)]
    merged = jnp.concatenate(
        [jnp.concatenate([att_recv[g, i] for g in range(NX)], axis=1) for i in range(2)], axis=0
    )
    base = jnp.concatenate([rres[g, pl.ds(i * 4, 4)].reshape(64, D) for i, g in both], axis=0)
    resid = (base.astype(jnp.float32) + dot32(merged, wo_ref[...])).astype(jnp.bfloat16)
    mlp_in = rms_rows(resid)

    def hidden(f, total):
        cols = pl.ds(pl.multiple_of(f * 512, 512), 512)
        inner = jax.nn.gelu(dot32(mlp_in, up_ref[:, cols])).astype(jnp.bfloat16)
        return total + dot32(inner, down_ref[cols, :])

    done = lax.fori_loop(0, FF // 512, hidden, resid.astype(jnp.float32), unroll=2)
    done = done.astype(jnp.bfloat16).reshape(2, NX, 4, PIECE, D)
    for i, g in both:
        for s in range(4):
            out_ref[i, s, g] = done[i, g, s]

    @pl.loop(1, NZ)
    def _(r):
        leaf_z(r).wait_send()
        pool_to_z(r).wait_send()

    @pl.loop(0, NZ)
    def _(r):
        @pl.loop(1, NS)
        def _(o):
            leaf_s(r, o).wait_send()
            sel_s(r, o).wait_send()

    @pl.loop(1, NS)
    def _(o):
        pool_to_s(o).wait_send()

    @pl.loop(1, NX)
    def _(o):
        weights(o).wait_send()
        for q in range(4):
            qkv_x(o, q).wait_send()
        resid_x(o).wait_send()
        att_x(o, 0).wait_send()
        att_x(o, 1).wait_send()

    for way in range(2):
        for step in range(4):
            for part in range(2):
                if step < 3 or part == way:
                    hop(way, step, part).wait_send()


def on_device(
    particles, query_weight, key_weight, value_weight, out_weight, up_weight, down_weight,
    rotated_slot, selected,
):
    bf, f32 = jnp.bfloat16, jnp.float32
    vmem = pl.BlockSpec(memory_space=pltpu.VMEM)
    hbm = pl.BlockSpec(memory_space=pl.ANY)
    sem = pltpu.SemaphoreType.DMA
    kv = pltpu.VMEM((8, 2 * HEAD, BALL), bf)
    result = pl.pallas_call(
        kernel,
        name="layer",
        out_shape=jax.ShapeDtypeStruct((2, 4, NX, PIECE, D), bf),
        in_specs=[hbm] * 9,
        out_specs=vmem,
        scratch_shapes=[
            pltpu.VMEM((16, 128), jnp.int32), pltpu.VMEM((TOPK, 512), jnp.int32),
            pltpu.VMEM((D, 128), bf), pltpu.VMEM((128, PIECE, D), bf),
            pltpu.VMEM((D, D), bf), pltpu.VMEM((D, FF), bf), pltpu.VMEM((FF, D), bf),
            pltpu.VMEM((NX, 192, D), bf),
            pltpu.VMEM((16, 128), jnp.int32),
            pltpu.SMEM((8, 128), jnp.int32), pltpu.SMEM((8, 128), jnp.int32),
            pltpu.VMEM((NZ, NS, PIECE, D), bf), pltpu.VMEM((NZ, NS, PIECE, D), bf),
            pltpu.VMEM((NS * NZ, PIECE, D), bf), pltpu.VMEM((32, PIECE, D), bf),
            pltpu.VMEM((NX, 4, 192, 128), bf), pltpu.VMEM((NX, 4, 192, 128), bf),
            pltpu.VMEM((NX, 8, PIECE, D), bf),
            kv, kv, kv, kv, kv, kv, kv, kv,
            pltpu.VMEM((NZ, NS, 2 * HEAD, BALL), bf),
            pltpu.VMEM((NS * NZ, 2 * HEAD, BALL), bf),
            pltpu.VMEM((8, 128), f32), pltpu.VMEM((NZ, 8, 128), f32),
            pltpu.VMEM((NS, NZ, 8, 128), f32),
            pltpu.VMEM((2, 3 * BALL, HEAD), bf), pltpu.VMEM((2, 2 * HEAD, 3 * BALL), bf),
            pltpu.VMEM((2, 3 * BALL, HEAD), bf), pltpu.VMEM((2, 2 * HEAD, 3 * BALL), bf),
            pltpu.VMEM((8, 128, BALL), f32), pltpu.VMEM((8, 128, BALL), f32),
            pltpu.VMEM((8, 8, BALL), f32), pltpu.VMEM((8, 128, BALL), bf),
            pltpu.VMEM((2, 3 * BALL, BALL), f32),
            pltpu.VMEM((8, BALL, 128), bf), pltpu.VMEM((NX, 2, BALL, 128), bf),
            sem((11,)), sem((NX,)), sem((NX,)), sem((NZ,)), sem((NZ,)),
            sem((NZ, NS)), sem((NZ, NS)), sem((NX, 4)), sem((NX, 4)), sem((NX,)), sem((NX,)),
            sem((2, 4, 2)), sem((2, 4, 2)), sem((NZ, NS)), sem((NZ, NS)), sem((NZ,)), sem((NZ,)),
            sem((NS,)), sem((NS,)), sem((NX, 2)), sem((NX, 2)),
        ],
        compiler_params=pltpu.CompilerParams(
            collective_id=0, has_side_effects=True, vmem_limit_bytes=60 * 1024 * 1024
        ),
    )(
        rotated_slot.reshape(16, 128), selected.T, query_weight, key_weight.T, value_weight.T,
        particles.reshape(128, PIECE, D), out_weight, up_weight, down_weight,
    )
    return result.reshape(512, D)


def solution(mesh):
    in_specs = (
        P("balls", None), P(None, "heads"), P(None, "heads"), P(None, "heads"),
        P(), P(), P(), P(), P(),
    )
    out_specs = P(("balls", "heads"), None)
    return jax.shard_map(
        on_device, mesh=mesh, in_specs=in_specs, out_specs=out_specs, check_vma=False
    )
```

```python
import functools
import math

import jax
import jax.numpy as jnp
from jax import lax
from jax.experimental import pallas as pl
from jax.experimental.pallas import tpu as pltpu
from jax.sharding import PartitionSpec as P

HEAD = 32
BALL = 256
LEAF = 64
TOPK = 3
NX, NY, NZ, NC = 4, 4, 8, 2
NS = NY * NC
PIECE = LEAF // NX
D = 512
FF = 2048
SCALE = math.log2(math.e) / math.sqrt(HEAD)
NT = (((1,), (1,)), ((), ()))
Z_ORDER = (4, 5, 3, 6, 2, 7, 1)


def rms_rows(matrix):
    wide = matrix.astype(jnp.float32)
    return (wide * lax.rsqrt(jnp.mean(wide * wide, axis=-1, keepdims=True) + 1e-05)).astype(
        jnp.bfloat16
    )


def dot32(left, right, dims=None):
    if dims is None:
        return jnp.dot(left, right, preferred_element_type=jnp.float32)
    return lax.dot_general(left, right, dims, preferred_element_type=jnp.float32)


def kernel(
    rs_hbm, sel_hbm, wq_hbm, wk_hbm, wv_hbm, p_hbm, wo_hbm, up_hbm, down_hbm, out_ref,
    rs_ref, sel_ref, wq_ref, p_ref, wo_ref, up_ref, down_ref, w_all,
    tab_v, tab_a, tab_b,
    leaf_stage, leaf_mid, leaf_recv, rotq, q_stage, q_recv, rres,
    k_own, k_p1, k_p2, k_p3, k_m1, k_m2, k_m3, k_4,
    v_own, v_p1, v_p2, v_p3, v_m1, v_m2, v_m3, v_4,
    sel_stage, sel_recv, pool_own, pool_z, pool_all,
    k_a, vt_a, k_b, vt_b, values, counts, tops, queries, score_buf, att_st, att_recv,
    load_sem, ws, wr, lzs, lzr, lss, lsr, xs, xr, rs, rr,
    ags, agr, sss, ssr, pzs, pzr, pss, psr, ats, atr,
):
    b = lax.axis_index("balls")
    h = lax.axis_index("heads")
    y = b // (NZ * NC)
    z = (b // NC) % NZ
    c = b % NC
    k = y * NC + c

    def z_peer(r):
        return {"balls": (y * NZ + (z + r) % NZ) * NC + c, "heads": h}

    def s_peer(o):
        kk = (k + o) % NS
        return {"balls": ((kk // NC) * NZ + z) * NC + kk % NC, "heads": h}

    def x_peer(o):
        return {"balls": b, "heads": (h + o) % NX}

    def remote(src, dst, send, recv, peer):
        return pltpu.make_async_remote_copy(
            src_ref=src, dst_ref=dst, send_sem=send, recv_sem=recv,
            device_id=peer, device_id_type=pl.DeviceIdType.MESH,
        )

    def all_sent(bulk, send):
        remote(bulk, bulk, send, send, x_peer(1)).wait_send()

    def all_here(bulk, recv):
        remote(bulk, bulk, recv, recv, x_peer(1)).wait_recv()

    barrier = pltpu.get_barrier_semaphore()

    @pl.loop(1, NZ)
    def _(r):
        pl.semaphore_signal(barrier, 1, device_id=z_peer(r))

    @pl.loop(1, NS)
    def _(o):
        pl.semaphore_signal(barrier, 1, device_id=s_peer(o))

    @pl.loop(1, NX)
    def _(o):
        pl.semaphore_signal(barrier, 1, device_id=x_peer(o))

    small = [
        pltpu.make_async_copy(rs_hbm, rs_ref, load_sem.at[6]),
        pltpu.make_async_copy(sel_hbm, sel_ref, load_sem.at[7]),
        pltpu.make_async_copy(wq_hbm, wq_ref, load_sem.at[8]),
        pltpu.make_async_copy(wk_hbm, w_all.at[h, pl.ds(128, HEAD)], load_sem.at[9]),
        pltpu.make_async_copy(wv_hbm, w_all.at[h, pl.ds(160, HEAD)], load_sem.at[10]),
    ]
    load_p = pltpu.make_async_copy(p_hbm, p_ref, load_sem.at[0])
    small[0].start()
    load_p.start()
    for load in small[1:]:
        load.start()
    loads = [
        pltpu.make_async_copy(wo_hbm, wo_ref, load_sem.at[1]),
        pltpu.make_async_copy(up_hbm, up_ref, load_sem.at[2]),
        pltpu.make_async_copy(down_hbm, down_ref, load_sem.at[3]),
    ]

    def iota(shape, axis):
        return lax.broadcasted_iota(jnp.int32, shape, axis)

    def slot(dev):
        return (((dev >> 4) * NC + (dev & 1)) << 3) + ((dev >> 1) & 7)

    def device(kk, zz):
        return (((kk >> 1) << 3) + zz) * NC + (kk & 1)

    def table(parts, at, target, which):
        used = sum(part.shape[0] for part in parts)
        if used < 128:
            parts = parts + [jnp.zeros((128 - used, 128), jnp.int32)]
        square = jnp.concatenate(parts, axis=0)
        tab_v[pl.ds(8 * at, 8)] = jnp.broadcast_to(
            jnp.max(square.T, axis=0, keepdims=True) & 63, (8, 128)
        )
        copy = pltpu.make_async_copy(tab_v.at[pl.ds(8 * at, 8)], target, load_sem.at[which])
        copy.start()
        return copy

    i64, lane64 = iota((64, 128), 0), iota((64, 128), 1)
    small[0].wait()
    own_row = rs_ref[pl.ds(b // 4, 1), :]
    found = ((own_row >> 5) == device(i64 & 7, i64 >> 3)) & ((lane64 >> 5) == b % 4)
    send = jnp.where(found, lane64 & 31, 0)
    table_a = table([send], 0, tab_a, 4)

    def selected_tables():
        place, lane = iota((32, 128), 0) + b * 32, iota((32, 128), 1)
        take = jnp.zeros((32, 128), jnp.int32)
        for row in range(16):
            found = rs_ref[pl.ds(row, 1), :] == place
            take = jnp.maximum(take, jnp.where(found, slot(row * 4 + (lane >> 5)), 0))
        i, ball = iota((64, 512), 0), iota((64, 512), 1)
        reader = (ball >> 3) == device(i & 7, z)
        origin = (y * NZ + (i >> 3)) * NC + c
        e, ball_e = iota((32, 512), 0), iota((32, 512), 1)
        give = jnp.zeros((64, 512), jnp.int32)
        fetch = jnp.zeros((32, 512), jnp.int32)
        for t in range(TOPK):
            pick = sel_ref[pl.ds(t, 1), :]
            give = jnp.maximum(give, jnp.where(reader & ((pick >> 3) == origin), pick & 7, 0))
            mine = (ball_e - b * 8) * TOPK + t == e
            fetch = jnp.maximum(fetch, jnp.where(mine, slot(pick >> 3), 0))
        give = functools.reduce(jnp.maximum, [give[:, 128 * q : 128 * q + 128] for q in range(4)])
        fetch = functools.reduce(jnp.maximum, [fetch[:, 128 * q : 128 * q + 128] for q in range(4)])
        return table([give, take, fetch], 1, tab_b, 5)

    load_p.wait()
    table_a.wait()

    @pl.loop(0, NZ)
    def _(zd):
        for kk in range(NS):
            leaf_stage[zd, kk] = p_ref[tab_a[0, zd * NS + kk] * NX + h]

    leaf_mid[z] = leaf_stage[z]
    for load in loads:
        load.start()
    for load in small[1:]:
        load.wait()
    w_all[h, pl.ds(0, 128)] = wq_ref[...].astype(jnp.float32).T.astype(jnp.bfloat16)
    table_b = selected_tables()
    pl.semaphore_wait(barrier, (NZ - 1) + (NS - 1) + (NX - 1))

    def leaf_z(r):
        return remote(
            leaf_stage.at[(z + r) % NZ], leaf_mid.at[z], lzs, lzr.at[r], z_peer(r)
        )

    for r in Z_ORDER:
        leaf_z(r).start()

    def weights(o):
        return remote(w_all.at[h], w_all.at[h], ws, wr, x_peer(o))

    @pl.loop(1, NX)
    def _(o):
        weights(o).start()

    ones8 = jnp.ones((8, BALL), jnp.bfloat16)
    row8 = iota((8, 2 * HEAD), 0)

    def own_ball(i, pooled):
        rows = p_ref[pl.ds(i * 16, 16)].reshape(BALL, D)
        kvt = dot32(w_all[h, pl.ds(128, 2 * HEAD)], rms_rows(rows), NT).astype(jnp.bfloat16)
        k_own[i] = kvt[:HEAD]
        v_own[i] = kvt[HEAD:]
        total = dot32(ones8, kvt, NT) * (1.0 / math.sqrt(BALL))
        return jnp.where(row8 == i, total.astype(jnp.bfloat16).astype(jnp.float32), pooled)

    pooled = lax.fori_loop(0, 8, own_ball, jnp.zeros((8, 2 * HEAD), jnp.float32))
    pool_own[...] = jnp.concatenate([pooled, jnp.zeros((8, 2 * HEAD), jnp.float32)], axis=1)

    def pool_to_z(r):
        return remote(pool_own, pool_z.at[z], pzs, pzr, z_peer(r))

    @pl.loop(1, NZ)
    def _(r):
        pool_to_z(r).start()

    rings = (
        ((k_own, k_p1, k_p2, k_p3, k_4), (k_own, k_m1, k_m2, k_m3, k_4)),
        ((v_own, v_p1, v_p2, v_p3, v_4), (v_own, v_m1, v_m2, v_m3, v_4)),
    )

    def hop(way, step, part):
        return remote(
            rings[part][way][step], rings[part][way][step + 1],
            ags, agr.at[way, step, part], z_peer(1 if way == 0 else NZ - 1),
        )

    for part in range(2):
        hop(0, 0, part).start()
        hop(1, 0, part).start()

    pool_z[z] = pool_own[...]

    table_b.wait()

    def forward(part, source, r):
        zs = (z + NZ - r) % NZ
        first = part * 64

        @pl.loop(0, NS)
        def _(kk):
            sel_stage[first + r * NS + kk] = source[tab_b[0, zs * NS + kk]]

        sel_recv[first + k * NZ + zs] = sel_stage[first + r * NS + k]

        @pl.loop(1, NS)
        def _(o):
            remote(
                sel_stage.at[first + r * NS + (k + o) % NS], sel_recv.at[first + k * NZ + zs],
                sss, ssr, s_peer(o),
            ).start()

    def relay(step, part):
        for way in range(2):
            hop(way, step - 1, part).wait_recv()
            if step < 3 or part == way:
                hop(way, step, part).start()
        forward(part, rings[part][0][step], step)
        forward(part, rings[part][1][step], NZ - step)

    forward(0, k_own, 0)
    forward(1, v_own, 0)

    for vt in (vt_a, vt_b):
        for i in range(2):
            vt[i, pl.ds(HEAD, HEAD), :] = jnp.ones((HEAD, 3 * BALL), jnp.bfloat16)

    def place(keys, vt, i, block, key_t, value_t):
        at = pl.ds(block * BALL, key_t.shape[1])
        keys[i, at, :] = key_t.astype(jnp.float32).T.astype(jnp.bfloat16)
        vt[i, pl.ds(0, HEAD), at] = value_t.astype(jnp.bfloat16)

    def leaf_s(r, o):
        zs = (z + NZ - r) % NZ
        kk = (k + o) % NS
        return remote(
            leaf_mid.at[zs, kk], leaf_recv.at[k * NZ + zs], lss, lsr, s_peer(o)
        )

    for r in (0,) + Z_ORDER:
        if r > 0:
            leaf_z(r).wait_recv()

        @pl.loop(1, NS)
        def _(o):
            leaf_s(r, o).start()

        zs = (z + NZ - r) % NZ
        leaf_recv[k * NZ + zs] = leaf_mid[zs, k]

    def pool_to_s(o):
        return remote(pool_z, pool_all.at[k], pss, psr, s_peer(o))

    all_here(pool_z.at[pl.ds(0, NZ - 1)], pzr)

    @pl.loop(1, NS)
    def _(o):
        pool_to_s(o).start()

    pool_all[k] = pool_z[...]

    relay(1, 0)

    all_here(w_all.at[pl.ds(0, NX - 1)], wr)
    all_here(leaf_recv.at[pl.ds(0, NZ * (NS - 1))], lsr)

    def qkv_x(o, q):
        return remote(
            q_stage.at[(h + o) % NX, q], q_recv.at[h, q], xs, xr.at[q], x_peer(o)
        )

    def project(q):
        for s in range(8):
            rotq[q * 8 + s] = leaf_recv[tab_b[0, 64 + q * 8 + s]]
        rows = rms_rows(rotq[pl.ds(q * 8, 8)].reshape(128, D))
        for g in range(NX):
            q_stage[g, q] = dot32(w_all[g], rows, NT).astype(jnp.bfloat16)
        for o in (2, 1, 3):
            qkv_x(o, q).start()
        q_recv[h, q] = q_stage[h, q]

    def project_two(first):
        @pl.loop(first, first + 2)
        def _(q):
            project(q)

    project_two(0)
    relay(1, 1)
    project_two(2)
    relay(2, 0)

    def resid_x(o):
        return remote(
            rotq.at[pl.ds(((h + o) % NX) * 8, 8)], rres.at[h], rs, rr, x_peer(o)
        )

    rres[h] = rotq[pl.ds(h * 8, 8)]
    eye = (iota((2 * HEAD, 128), 0) == iota((2 * HEAD, 128), 1)).astype(jnp.bfloat16)

    all_here(pool_all.at[pl.ds(0, NS - 1)], psr)

    pool_rows = pool_all[...].reshape(2 * BALL, 128).astype(jnp.bfloat16)
    pool_t = dot32(eye, pool_rows, NT)
    for i in range(2):
        place(k_a, vt_a, i, 1, pool_t[:HEAD], pool_t[HEAD:])

    left = iota((128 + 2 * HEAD, 128), 1) < 64

    def transposed_rows(pair, i):
        tiles = [q_recv[g, pair] for g in range(NX)]
        rolled = [pltpu.roll(tile.astype(jnp.float32), 64, 1).astype(jnp.bfloat16) for tile in tiles]
        if i == 0:
            halves = [jnp.where(left, tiles[g], rolled[g + 1]) for g in (0, 2)]
        else:
            halves = [jnp.where(left, rolled[g], tiles[g + 1]) for g in (0, 2)]
        return jnp.concatenate(halves, axis=1)

    def run_heads(keys, vt, query, start, finish):
        blocks = [pl.ds(BALL * t, BALL) for t in range(3)]

        def scores(u, t, top):
            score = dot32(keys[u // 4, blocks[t], :], query(u))
            score_buf[u % 2, blocks[t], :] = score
            part = jnp.max(score.reshape(32, 8, BALL), axis=0)
            return part if top is None else jnp.maximum(top, part)

        upcoming = None
        for t in range(3):
            upcoming = scores(0, t, upcoming)
        for u in range(8):
            top = jnp.max(upcoming, axis=0, keepdims=True)
            before = start(u)
            if before is not None:
                top = jnp.maximum(top, before)
            upcoming, result = None, None
            for t in range(3):
                if u < 7:
                    upcoming = scores(u + 1, t, upcoming)
                weight = jnp.exp2((score_buf[u % 2, blocks[t], :] - top) * SCALE)
                part = dot32(vt[u // 4, :, blocks[t]], weight.astype(jnp.bfloat16))
                result = part if result is None else result + part
            finish(u, result[:HEAD], result[HEAD:], top, before)

    def attend_own(pair):
        for i in range(2):
            rows = transposed_rows(pair, i)
            queries[pair * 2 + i] = rows[:128]
            place(k_a, vt_a, i, 0, rows[128:160], rows[160:])

        def query(u):
            return queries[pair * 2 + u // 4, pl.ds(HEAD * (u % 4), HEAD)]

        def finish(u, value, count, top, before):
            ball, j = pair * 2 + u // 4, u % 4
            values[ball, pl.ds(HEAD * j, HEAD)] = value
            counts[ball, pl.ds(HEAD * j, HEAD)] = count
            tops[ball, pl.ds(j, 1)] = top

        run_heads(k_a, vt_a, query, lambda u: None, finish)

    def attend_selected(pair, ready):
        for i in range(2):
            for t in range(TOPK):
                at = tab_b[0, 96 + (pair * 2 + i) * TOPK + t]
                place(k_b, vt_b, i, t, sel_recv[at], sel_recv[64 + at])

        def query(u):
            return queries[pair * 2 + u // 4, pl.ds(HEAD * (u % 4), HEAD)]

        def start(u):
            return tops[pair * 2 + u // 4, pl.ds(u % 4, 1)]

        parts = []

        def finish(u, value, count, top, before):
            ball, at = pair * 2 + u // 4, pl.ds(HEAD * (u % 4), HEAD)
            scale = jnp.exp2((before - top) * SCALE)
            parts.append((value + values[ball, at] * scale) / (count + counts[ball, at] * scale))
            if u % 4 == 3:
                att_st[ball] = jnp.concatenate(parts[u - 3 :], axis=0).T.astype(jnp.bfloat16)
                ready(u // 4)

        run_heads(k_b, vt_b, query, start, finish)

    def own_pair(pair):
        all_here(q_stage.at[0, pl.ds(0, NX - 1)], xr.at[pair])
        attend_own(pair)

    @pl.loop(0, NX)
    def _(pair):
        own_pair(pair)

        @pl.when(pair == 0)
        def _():
            relay(2, 1)

        @pl.when(pair == 1)
        def _():
            relay(3, 0)

        @pl.when(pair == 2)
        def _():
            relay(3, 1)

            @pl.loop(1, NX)
            def _(o):
                resid_x(o).start()

    hop(0, 3, 0).wait_recv()
    forward(0, k_4, 4)
    hop(1, 3, 1).wait_recv()
    forward(1, v_4, 4)
    all_here(sel_recv.at[pl.ds(0, 2 * NZ * (NS - 1))], ssr)

    def att_x(o, i):
        return remote(
            att_st.at[((h + o) % NX) * 2 + i], att_recv.at[h, i], ats, atr, x_peer(o)
        )

    @pl.loop(1, NX)
    def _(o):
        attend_selected((h + o) % NX, lambda i: att_x(o, i).start())

    attend_selected(h, lambda i: None)
    att_recv[h] = att_st[pl.ds(h * 2, 2)]

    for load in loads:
        load.wait()

    all_here(rres.at[pl.ds(0, NX - 1)], rr)
    all_here(att_st.at[pl.ds(0, 2 * (NX - 1))], atr)
    both = [(i, g) for i in range(2) for g in range(NX)]
    merged = jnp.concatenate(
        [jnp.concatenate([att_recv[g, i] for g in range(NX)], axis=1) for i in range(2)], axis=0
    )
    base = jnp.concatenate([rres[g, pl.ds(i * 4, 4)].reshape(64, D) for i, g in both], axis=0)
    resid = (base.astype(jnp.float32) + dot32(merged, wo_ref[...])).astype(jnp.bfloat16)
    mlp_in = rms_rows(resid)

    def hidden(f, total):
        cols = pl.ds(pl.multiple_of(f * 512, 512), 512)
        inner = jax.nn.gelu(dot32(mlp_in, up_ref[:, cols])).astype(jnp.bfloat16)
        return total + dot32(inner, down_ref[cols, :])

    done = lax.fori_loop(0, FF // 512, hidden, resid.astype(jnp.float32), unroll=2)
    done = done.astype(jnp.bfloat16).reshape(2, NX, 4, PIECE, D)
    for i, g in both:
        for s in range(4):
            out_ref[i, s, g] = done[i, g, s]

    all_sent(leaf_stage.at[pl.ds(0, NZ - 1)], lzs)
    all_sent(leaf_recv.at[pl.ds(0, NZ * (NS - 1))], lss)
    all_sent(pool_z.at[pl.ds(0, NZ - 1)], pzs)
    all_sent(pool_all.at[pl.ds(0, NS - 1)], pss)
    all_sent(w_all.at[pl.ds(0, NX - 1)], ws)
    all_sent(q_stage.at[pl.ds(0, NX - 1)], xs)
    all_sent(rres.at[pl.ds(0, NX - 1)], rs)
    all_sent(att_st.at[pl.ds(0, 2 * (NX - 1))], ats)
    all_sent(sel_stage.at[pl.ds(0, 2 * 7 * NS)], ags)
    all_sent(sel_recv.at[pl.ds(0, 2 * NZ * (NS - 1))], sss)


def on_device(
    particles, query_weight, key_weight, value_weight, out_weight, up_weight, down_weight,
    rotated_slot, selected,
):
    bf, f32 = jnp.bfloat16, jnp.float32
    vmem = pl.BlockSpec(memory_space=pltpu.VMEM)
    hbm = pl.BlockSpec(memory_space=pl.ANY)
    sem = pltpu.SemaphoreType.DMA
    ball_rows = pltpu.VMEM((8, HEAD, BALL), bf)
    result = pl.pallas_call(
        kernel,
        name="layer",
        out_shape=jax.ShapeDtypeStruct((2, 4, NX, PIECE, D), bf),
        in_specs=[hbm] * 9,
        out_specs=vmem,
        scratch_shapes=[
            pltpu.VMEM((16, 128), jnp.int32), pltpu.VMEM((TOPK, 512), jnp.int32),
            pltpu.VMEM((D, 128), bf), pltpu.VMEM((128, PIECE, D), bf),
            pltpu.VMEM((D, D), bf), pltpu.VMEM((D, FF), bf), pltpu.VMEM((FF, D), bf),
            pltpu.VMEM((NX, 192, D), bf),
            pltpu.VMEM((16, 128), jnp.int32),
            pltpu.SMEM((8, 128), jnp.int32), pltpu.SMEM((8, 128), jnp.int32),
            pltpu.VMEM((NZ, NS, PIECE, D), bf), pltpu.VMEM((NZ, NS, PIECE, D), bf),
            pltpu.VMEM((NS * NZ, PIECE, D), bf), pltpu.VMEM((32, PIECE, D), bf),
            pltpu.VMEM((NX, 4, 192, 128), bf), pltpu.VMEM((NX, 4, 192, 128), bf),
            pltpu.VMEM((NX, 8, PIECE, D), bf),
            *([ball_rows] * 16),
            pltpu.VMEM((2 * NZ * NS, HEAD, BALL), bf),
            pltpu.VMEM((2 * NS * NZ, HEAD, BALL), bf),
            pltpu.VMEM((8, 128), f32), pltpu.VMEM((NZ, 8, 128), f32),
            pltpu.VMEM((NS, NZ, 8, 128), f32),
            pltpu.VMEM((2, 3 * BALL, HEAD), bf), pltpu.VMEM((2, 2 * HEAD, 3 * BALL), bf),
            pltpu.VMEM((2, 3 * BALL, HEAD), bf), pltpu.VMEM((2, 2 * HEAD, 3 * BALL), bf),
            pltpu.VMEM((8, 128, BALL), f32), pltpu.VMEM((8, 128, BALL), f32),
            pltpu.VMEM((8, 8, BALL), f32), pltpu.VMEM((8, 128, BALL), bf),
            pltpu.VMEM((2, 3 * BALL, BALL), f32),
            pltpu.VMEM((8, BALL, 128), bf), pltpu.VMEM((NX, 2, BALL, 128), bf),
            sem((11,)), sem, sem, sem, sem((NZ,)), sem, sem, sem, sem((4,)), sem, sem,
            sem, sem((2, 4, 2)), sem, sem, sem, sem, sem, sem, sem, sem,
        ],
        compiler_params=pltpu.CompilerParams(
            collective_id=0, has_side_effects=True, vmem_limit_bytes=60 * 1024 * 1024
        ),
    )(
        rotated_slot.reshape(16, 128), selected.T, query_weight, key_weight.T, value_weight.T,
        particles.reshape(128, PIECE, D), out_weight, up_weight, down_weight,
    )
    return result.reshape(512, D)


def solution(mesh):
    in_specs = (
        P("balls", None), P(None, "heads"), P(None, "heads"), P(None, "heads"),
        P(), P(), P(), P(), P(),
    )
    out_specs = P(("balls", "heads"), None)
    return jax.shard_map(
        on_device, mesh=mesh, in_specs=in_specs, out_specs=out_specs, check_vma=False
    )
```

```python
import functools
import math

import jax
import jax.numpy as jnp
from jax import lax
from jax.experimental import pallas as pl
from jax.experimental.pallas import tpu as pltpu
from jax.sharding import PartitionSpec as P

HEAD = 32
BALL = 256
LEAF = 64
TOPK = 3
NX, NY, NZ, NC = 4, 4, 8, 2
NS = NY * NC
PIECE = LEAF // NX
D = 512
FF = 2048
SCALE = math.log2(math.e) / math.sqrt(HEAD)
NT = (((1,), (1,)), ((), ()))
Z_ORDER = (4, 5, 3, 6, 2, 7, 1)


def rms_rows(matrix):
    wide = matrix.astype(jnp.float32)
    return (wide * lax.rsqrt(jnp.mean(wide * wide, axis=-1, keepdims=True) + 1e-05)).astype(
        jnp.bfloat16
    )


def dot32(left, right, dims=None):
    if dims is None:
        return jnp.dot(left, right, preferred_element_type=jnp.float32)
    return lax.dot_general(left, right, dims, preferred_element_type=jnp.float32)


def kernel(
    rs_hbm, sel_hbm, wq_hbm, wk_hbm, wv_hbm, p_hbm, wo_hbm, up_hbm, down_hbm, out_any,
    out_ref,    rs_ref, sel_ref, wq_ref, p_ref, wo_ref, up_ref, down_ref, w_all,
    tab_v, tab_a, tab_b,
    leaf_stage, leaf_mid, leaf_recv, rotq, q_stage, q_recv, rres,
    k_own, k_p1, k_p2, k_p3, k_m1, k_m2, k_m3, k_4,
    v_own, v_p1, v_p2, v_p3, v_m1, v_m2, v_m3, v_4,
    sel_stage, sel_k, sel_v, pool_own, pool_z, pool_all,
    k_a, vt_a, k_b, values, counts, tops, queries, score_buf, att_st, att_recv,
    load_sem, ws, wr, lzs, lzr, lss, lsr, xs, xr, rs, rr,
    ags, agr, sss, ssr_k, ssr_v, pzs, pzr, pss, psr, ats, atr,
):
    b = lax.axis_index("balls")
    h = lax.axis_index("heads")
    y = b // (NZ * NC)
    z = (b // NC) % NZ
    c = b % NC
    k = y * NC + c

    def z_peer(r):
        return {"balls": (y * NZ + (z + r) % NZ) * NC + c, "heads": h}

    def s_peer(o):
        kk = (k + o) % NS
        return {"balls": ((kk // NC) * NZ + z) * NC + kk % NC, "heads": h}

    def x_peer(o):
        return {"balls": b, "heads": (h + o) % NX}

    def remote(src, dst, send, recv, peer):
        return pltpu.make_async_remote_copy(
            src_ref=src, dst_ref=dst, send_sem=send, recv_sem=recv,
            device_id=peer, device_id_type=pl.DeviceIdType.MESH,
        )

    def all_sent(bulk, send):
        remote(bulk, bulk, send, send, x_peer(1)).wait_send()

    def all_here(bulk, recv):
        remote(bulk, bulk, recv, recv, x_peer(1)).wait_recv()

    barrier = pltpu.get_barrier_semaphore()

    @pl.loop(1, NZ)
    def _(r):
        pl.semaphore_signal(barrier, 1, device_id=z_peer(r))

    @pl.loop(1, NS)
    def _(o):
        pl.semaphore_signal(barrier, 1, device_id=s_peer(o))

    @pl.loop(1, NX)
    def _(o):
        pl.semaphore_signal(barrier, 1, device_id=x_peer(o))

    small = [
        pltpu.make_async_copy(rs_hbm, rs_ref, load_sem.at[6]),
        pltpu.make_async_copy(sel_hbm, sel_ref, load_sem.at[7]),
        pltpu.make_async_copy(wq_hbm, wq_ref, load_sem.at[8]),
        pltpu.make_async_copy(wk_hbm, w_all.at[h, pl.ds(128, HEAD)], load_sem.at[9]),
        pltpu.make_async_copy(wv_hbm, w_all.at[h, pl.ds(160, HEAD)], load_sem.at[10]),
    ]
    load_p = pltpu.make_async_copy(p_hbm, p_ref, load_sem.at[0])
    small[0].start()
    load_p.start()
    for load in small[1:]:
        load.start()
    loads = [
        pltpu.make_async_copy(wo_hbm, wo_ref, load_sem.at[1]),
        pltpu.make_async_copy(up_hbm, up_ref, load_sem.at[2]),
        pltpu.make_async_copy(down_hbm, down_ref, load_sem.at[3]),
    ]

    def iota(shape, axis):
        return lax.broadcasted_iota(jnp.int32, shape, axis)

    def slot(dev):
        return (((dev >> 4) * NC + (dev & 1)) << 3) + ((dev >> 1) & 7)

    def device(kk, zz):
        return (((kk >> 1) << 3) + zz) * NC + (kk & 1)

    def table(parts, at, target, which):
        used = sum(part.shape[0] for part in parts)
        if used < 128:
            parts = parts + [jnp.zeros((128 - used, 128), jnp.int32)]
        square = jnp.concatenate(parts, axis=0)
        tab_v[pl.ds(8 * at, 8)] = jnp.broadcast_to(
            jnp.max(square.T, axis=0, keepdims=True) & 63, (8, 128)
        )
        copy = pltpu.make_async_copy(tab_v.at[pl.ds(8 * at, 8)], target, load_sem.at[which])
        copy.start()
        return copy

    i64, lane64 = iota((64, 128), 0), iota((64, 128), 1)
    small[0].wait()
    own_row = rs_ref[pl.ds(b // 4, 1), :]
    found = ((own_row >> 5) == device(i64 & 7, i64 >> 3)) & ((lane64 >> 5) == b % 4)
    send = jnp.where(found, lane64 & 31, 0)
    table_a = table([send], 0, tab_a, 4)

    def selected_tables():
        place, lane = iota((32, 128), 0) + b * 32, iota((32, 128), 1)
        take = jnp.zeros((32, 128), jnp.int32)
        for row in range(16):
            found = rs_ref[pl.ds(row, 1), :] == place
            take = jnp.maximum(take, jnp.where(found, slot(row * 4 + (lane >> 5)), 0))
        i, ball = iota((64, 512), 0), iota((64, 512), 1)
        reader = (ball >> 3) == device(i & 7, z)
        origin = (y * NZ + (i >> 3)) * NC + c
        e, ball_e = iota((32, 512), 0), iota((32, 512), 1)
        give = jnp.zeros((64, 512), jnp.int32)
        fetch = jnp.zeros((32, 512), jnp.int32)
        for t in range(TOPK):
            pick = sel_ref[pl.ds(t, 1), :]
            give = jnp.maximum(give, jnp.where(reader & ((pick >> 3) == origin), pick & 7, 0))
            mine = (ball_e - b * 8) * TOPK + t == e
            fetch = jnp.maximum(fetch, jnp.where(mine, slot(pick >> 3), 0))
        give = functools.reduce(jnp.maximum, [give[:, 128 * q : 128 * q + 128] for q in range(4)])
        fetch = functools.reduce(jnp.maximum, [fetch[:, 128 * q : 128 * q + 128] for q in range(4)])
        return table([give, take, fetch], 1, tab_b, 5)

    load_p.wait()
    table_a.wait()

    @pl.loop(0, NZ)
    def _(zd):
        for kk in range(NS):
            leaf_stage[zd, kk] = p_ref[tab_a[0, zd * NS + kk] * NX + h]

    leaf_mid[z] = leaf_stage[z]
    for load in loads:
        load.start()
    for load in small[1:]:
        load.wait()
    w_all[h, pl.ds(0, 128)] = wq_ref[...].astype(jnp.float32).T.astype(jnp.bfloat16)
    table_b = selected_tables()
    pl.semaphore_wait(barrier, (NZ - 1) + (NS - 1) + (NX - 1))

    def leaf_z(r):
        return remote(
            leaf_stage.at[(z + r) % NZ], leaf_mid.at[z], lzs, lzr.at[r], z_peer(r)
        )

    for r in Z_ORDER:
        leaf_z(r).start()

    def weights(o):
        return remote(w_all.at[h], w_all.at[h], ws, wr, x_peer(o))

    @pl.loop(1, NX)
    def _(o):
        weights(o).start()

    ones8 = jnp.ones((8, BALL), jnp.bfloat16)
    row8 = iota((8, 2 * HEAD), 0)

    def own_ball(i, pooled):
        rows = p_ref[pl.ds(i * 16, 16)].reshape(BALL, D)
        kvt = dot32(w_all[h, pl.ds(128, 2 * HEAD)], rms_rows(rows), NT).astype(jnp.bfloat16)
        k_own[i] = kvt[:HEAD]
        v_own[i] = kvt[HEAD:]
        total = dot32(ones8, kvt, NT) * (1.0 / math.sqrt(BALL))
        return jnp.where(row8 == i, total.astype(jnp.bfloat16).astype(jnp.float32), pooled)

    pooled = lax.fori_loop(0, 8, own_ball, jnp.zeros((8, 2 * HEAD), jnp.float32))
    pool_own[...] = jnp.concatenate([pooled, jnp.zeros((8, 2 * HEAD), jnp.float32)], axis=1)

    def pool_to_z(r):
        return remote(pool_own, pool_z.at[z], pzs, pzr, z_peer(r))

    @pl.loop(1, NZ)
    def _(r):
        pool_to_z(r).start()

    rings = (
        ((k_own, k_p1, k_p2, k_p3, k_4), (k_own, k_m1, k_m2, k_m3, k_4)),
        ((v_own, v_p1, v_p2, v_p3, v_4), (v_own, v_m1, v_m2, v_m3, v_4)),
    )

    def hop(way, step, part):
        return remote(
            rings[part][way][step], rings[part][way][step + 1],
            ags, agr.at[way, step, part], z_peer(1 if way == 0 else NZ - 1),
        )

    for part in range(2):
        hop(0, 0, part).start()
        hop(1, 0, part).start()

    pool_z[z] = pool_own[...]

    table_b.wait()

    def forward(part, source, r):
        zs = (z + NZ - r) % NZ
        first = part * 64
        landing, arrived = ((sel_k, ssr_k), (sel_v, ssr_v))[part]

        @pl.loop(0, NS)
        def _(kk):
            sel_stage[first + r * NS + kk] = source[tab_b[0, zs * NS + kk]]

        landing[k * NZ + zs] = sel_stage[first + r * NS + k]

        @pl.loop(1, NS)
        def _(o):
            remote(
                sel_stage.at[first + r * NS + (k + o) % NS], landing.at[k * NZ + zs],
                sss, arrived, s_peer(o),
            ).start()

    def relay(step, part):
        for way in range(2):
            hop(way, step - 1, part).wait_recv()
            if step < 3 or part == way:
                hop(way, step, part).start()
        forward(part, rings[part][0][step], step)
        forward(part, rings[part][1][step], NZ - step)

    forward(0, k_own, 0)
    forward(1, v_own, 0)

    for i in range(2):
        vt_a[i, pl.ds(HEAD, HEAD), :] = jnp.ones((HEAD, 3 * BALL), jnp.bfloat16)

    def place(i, block, key_t, value_t):
        at = pl.ds(block * BALL, key_t.shape[1])
        k_a[i, at, :] = key_t.astype(jnp.float32).T.astype(jnp.bfloat16)
        vt_a[i, pl.ds(0, HEAD), at] = value_t.astype(jnp.bfloat16)

    def leaf_s(r, o):
        zs = (z + NZ - r) % NZ
        kk = (k + o) % NS
        return remote(
            leaf_mid.at[zs, kk], leaf_recv.at[k * NZ + zs], lss, lsr, s_peer(o)
        )

    for r in (0,) + Z_ORDER:
        if r > 0:
            leaf_z(r).wait_recv()

        @pl.loop(1, NS)
        def _(o):
            leaf_s(r, o).start()

        zs = (z + NZ - r) % NZ
        leaf_recv[k * NZ + zs] = leaf_mid[zs, k]

    def pool_to_s(o):
        return remote(pool_z, pool_all.at[k], pss, psr, s_peer(o))

    all_here(pool_z.at[pl.ds(0, NZ - 1)], pzr)

    @pl.loop(1, NS)
    def _(o):
        pool_to_s(o).start()

    pool_all[k] = pool_z[...]

    relay(1, 0)

    all_here(w_all.at[pl.ds(0, NX - 1)], wr)
    all_here(leaf_recv.at[pl.ds(0, NZ * (NS - 1))], lsr)

    def qkv_x(o, q):
        return remote(
            q_stage.at[(h + o) % NX, q], q_recv.at[h, q], xs, xr.at[q], x_peer(o)
        )

    def project(q):
        for s in range(8):
            rotq[q * 8 + s] = leaf_recv[tab_b[0, 64 + q * 8 + s]]
        rows = rms_rows(rotq[pl.ds(q * 8, 8)].reshape(128, D))
        for g in range(NX):
            q_stage[g, q] = dot32(w_all[g], rows, NT).astype(jnp.bfloat16)
        for o in (2, 1, 3):
            qkv_x(o, q).start()
        q_recv[h, q] = q_stage[h, q]

    def project_two(first):
        @pl.loop(first, first + 2)
        def _(q):
            project(q)

    project_two(0)
    relay(1, 1)
    project_two(2)
    relay(2, 0)

    def resid_x(o):
        return remote(
            rotq.at[pl.ds(((h + o) % NX) * 8, 8)], rres.at[h], rs, rr, x_peer(o)
        )

    rres[h] = rotq[pl.ds(h * 8, 8)]
    eye = (iota((2 * HEAD, 128), 0) == iota((2 * HEAD, 128), 1)).astype(jnp.bfloat16)

    all_here(pool_all.at[pl.ds(0, NS - 1)], psr)

    pool_rows = pool_all[...].reshape(2 * BALL, 128).astype(jnp.bfloat16)
    pool_t = dot32(eye, pool_rows, NT)
    for i in range(2):
        place(i, 1, pool_t[:HEAD], pool_t[HEAD:])

    left = iota((128 + 2 * HEAD, 128), 1) < 64

    def transposed_rows(pair, i):
        tiles = [q_recv[g, pair] for g in range(NX)]
        rolled = [pltpu.roll(tile.astype(jnp.float32), 64, 1).astype(jnp.bfloat16) for tile in tiles]
        if i == 0:
            halves = [jnp.where(left, tiles[g], rolled[g + 1]) for g in (0, 2)]
        else:
            halves = [jnp.where(left, rolled[g], tiles[g + 1]) for g in (0, 2)]
        return jnp.concatenate(halves, axis=1)

    blocks = [pl.ds(BALL * t, BALL) for t in range(3)]

    def run_heads(count, keys, vt, query, start, finish):
        def scores(u, t, top):
            score = dot32(keys(u, t), query(u))
            score_buf[u % 2, blocks[t], :] = score
            part = jnp.max(score.reshape(32, 8, BALL), axis=0)
            return part if top is None else jnp.maximum(top, part)

        upcoming = None
        for t in range(3):
            upcoming = scores(0, t, upcoming)
        for u in range(count):
            top = jnp.max(upcoming, axis=0, keepdims=True)
            before = start(u)
            if before is not None:
                top = jnp.maximum(top, before)
            upcoming, result = None, None
            for t in range(3):
                if u < count - 1:
                    upcoming = scores(u + 1, t, upcoming)
                weight = jnp.exp2((score_buf[u % 2, blocks[t], :] - top) * SCALE)
                part = dot32(vt(u, t), weight.astype(jnp.bfloat16))
                result = part if result is None else result + part
            finish(u, result[:HEAD], result[HEAD:], top, before)

    def attend_own(pair):
        for i in range(2):
            rows = transposed_rows(pair, i)
            queries[pair * 2 + i] = rows[:128]
            place(i, 0, rows[128:160], rows[160:])

        def query(u):
            return queries[pair * 2 + u // 4, pl.ds(HEAD * (u % 4), HEAD)]

        def finish(u, value, count, top, before):
            ball, j = pair * 2 + u // 4, u % 4
            values[ball, pl.ds(HEAD * j, HEAD)] = value
            counts[ball, pl.ds(HEAD * j, HEAD)] = count
            tops[ball, pl.ds(j, 1)] = top

        run_heads(
            8, lambda u, t: k_a[u // 4, blocks[t], :], lambda u, t: vt_a[u // 4, :, blocks[t]],
            query, lambda u: None, finish,
        )

    def attend_selected():
        ones = jnp.ones((HEAD, BALL), jnp.bfloat16)
        balls = [((h + 1 + n // 2) % NX) * 2 + n % 2 for n in range(8)]

        def keys(u, t):
            return k_b[balls[u // 4], blocks[t], :]

        def value_rows(u, t):
            at = tab_b[0, 96 + balls[u // 4] * TOPK + t]
            return jnp.concatenate([sel_v[at], ones], axis=0)

        def query(u):
            return queries[balls[u // 4], pl.ds(HEAD * (u % 4), HEAD)]

        def start(u):
            return tops[balls[u // 4], pl.ds(u % 4, 1)]

        parts = []

        def finish(u, value, count, top, before):
            n, at = u // 4, pl.ds(HEAD * (u % 4), HEAD)
            scale = jnp.exp2((before - top) * SCALE)
            value = value + values[balls[n], at] * scale
            parts.append(value / (count + counts[balls[n], at] * scale))
            if u % 4 == 3:
                att_st[balls[n]] = jnp.concatenate(parts[u - 3 :], axis=0).T.astype(jnp.bfloat16)
                if n < 6:
                    att_x(1 + n // 2, n % 2).start()

        run_heads(32, keys, value_rows, query, start, finish)

    def own_pair(pair):
        all_here(q_stage.at[0, pl.ds(0, NX - 1)], xr.at[pair])
        attend_own(pair)

    relay(2, 1)

    @pl.loop(0, NX)
    def _(pair):
        own_pair(pair)

        @pl.when(pair == 0)
        def _():
            relay(3, 0)

        @pl.when(pair == 1)
        def _():
            relay(3, 1)

            @pl.loop(1, NX)
            def _(o):
                resid_x(o).start()

        @pl.when(pair == 2)
        def _():
            hop(0, 3, 0).wait_recv()
            forward(0, k_4, 4)

    hop(1, 3, 1).wait_recv()
    forward(1, v_4, 4)
    all_here(sel_k.at[pl.ds(0, NZ * (NS - 1))], ssr_k)

    @pl.loop(0, 8)
    def _(ball):
        for t in range(TOPK):
            key_t = sel_k[tab_b[0, 96 + ball * TOPK + t]]
            k_b[ball, blocks[t], :] = key_t.astype(jnp.float32).T.astype(jnp.bfloat16)

    all_here(sel_v.at[pl.ds(0, NZ * (NS - 1))], ssr_v)

    def att_x(o, i):
        return remote(
            att_st.at[((h + o) % NX) * 2 + i], att_recv.at[h, i], ats, atr, x_peer(o)
        )

    attend_selected()
    att_recv[h] = att_st[pl.ds(h * 2, 2)]

    for load in loads:
        load.wait()

    all_here(rres.at[pl.ds(0, NX - 1)], rr)
    all_here(att_st.at[pl.ds(0, 2 * (NX - 1))], atr)
    both = [(i, g) for i in range(2) for g in range(NX)]
    merged = jnp.concatenate(
        [jnp.concatenate([att_recv[g, i] for g in range(NX)], axis=1) for i in range(2)], axis=0
    )
    base = jnp.concatenate([rres[g, pl.ds(i * 4, 4)].reshape(64, D) for i, g in both], axis=0)
    resid = (base.astype(jnp.float32) + dot32(merged, wo_ref[...])).astype(jnp.bfloat16)
    mlp_in = rms_rows(resid)

    def hidden(f, total):
        cols = pl.ds(pl.multiple_of(f * 512, 512), 512)
        inner = jax.nn.gelu(dot32(mlp_in, up_ref[:, cols])).astype(jnp.bfloat16)
        return total + dot32(inner, down_ref[cols, :])

    done = lax.fori_loop(0, FF // 512, hidden, resid.astype(jnp.float32), unroll=2)
    done = done.astype(jnp.bfloat16).reshape(2, NX, 4, PIECE, D)
    for i, g in both:
        for s in range(4):
            out_ref[i, s, g] = done[i, g, s]
    deliver = pltpu.make_async_copy(out_ref, out_any, load_sem.at[0])
    deliver.start()

    deliver.wait()
    all_sent(leaf_stage.at[pl.ds(0, NZ - 1)], lzs)
    all_sent(leaf_recv.at[pl.ds(0, NZ * (NS - 1))], lss)
    all_sent(pool_z.at[pl.ds(0, NZ - 1)], pzs)
    all_sent(pool_all.at[pl.ds(0, NS - 1)], pss)
    all_sent(w_all.at[pl.ds(0, NX - 1)], ws)
    all_sent(q_stage.at[pl.ds(0, NX - 1)], xs)
    all_sent(rres.at[pl.ds(0, NX - 1)], rs)
    all_sent(att_st.at[pl.ds(0, 2 * (NX - 1))], ats)
    all_sent(sel_stage.at[pl.ds(0, 2 * 7 * NS)], ags)
    all_sent(sel_stage.at[pl.ds(0, 2 * NZ * (NS - 1))], sss)


def on_device(
    particles, query_weight, key_weight, value_weight, out_weight, up_weight, down_weight,
    rotated_slot, selected,
):
    bf, f32 = jnp.bfloat16, jnp.float32
    hbm = pl.BlockSpec(memory_space=pl.ANY)
    sem = pltpu.SemaphoreType.DMA
    ball_rows = pltpu.VMEM((8, HEAD, BALL), bf)
    result = pl.pallas_call(
        kernel,
        name="layer",
        out_shape=pltpu.VMEM((2, 4, NX, PIECE, D), bf),
        in_specs=[hbm] * 9,
        out_specs=hbm,
        scratch_shapes=[
            pltpu.VMEM((2, 4, NX, PIECE, D), bf),
            pltpu.VMEM((16, 128), jnp.int32), pltpu.VMEM((TOPK, 512), jnp.int32),
            pltpu.VMEM((D, 128), bf), pltpu.VMEM((128, PIECE, D), bf),
            pltpu.VMEM((D, D), bf), pltpu.VMEM((D, FF), bf), pltpu.VMEM((FF, D), bf),
            pltpu.VMEM((NX, 192, D), bf),
            pltpu.VMEM((16, 128), jnp.int32),
            pltpu.SMEM((8, 128), jnp.int32), pltpu.SMEM((8, 128), jnp.int32),
            pltpu.VMEM((NZ, NS, PIECE, D), bf), pltpu.VMEM((NZ, NS, PIECE, D), bf),
            pltpu.VMEM((NS * NZ, PIECE, D), bf), pltpu.VMEM((32, PIECE, D), bf),
            pltpu.VMEM((NX, 4, 192, 128), bf), pltpu.VMEM((NX, 4, 192, 128), bf),
            pltpu.VMEM((NX, 8, PIECE, D), bf),
            *([ball_rows] * 16),
            pltpu.VMEM((2 * NZ * NS, HEAD, BALL), bf),
            pltpu.VMEM((NS * NZ, HEAD, BALL), bf), pltpu.VMEM((NS * NZ, HEAD, BALL), bf),
            pltpu.VMEM((8, 128), f32), pltpu.VMEM((NZ, 8, 128), f32),
            pltpu.VMEM((NS, NZ, 8, 128), f32),
            pltpu.VMEM((2, 3 * BALL, HEAD), bf), pltpu.VMEM((2, 2 * HEAD, 3 * BALL), bf),
            pltpu.VMEM((8, 3 * BALL, HEAD), bf),
            pltpu.VMEM((8, 128, BALL), f32), pltpu.VMEM((8, 128, BALL), f32),
            pltpu.VMEM((8, 8, BALL), f32), pltpu.VMEM((8, 128, BALL), bf),
            pltpu.VMEM((2, 3 * BALL, BALL), f32),
            pltpu.VMEM((8, BALL, 128), bf), pltpu.VMEM((NX, 2, BALL, 128), bf),
            sem((11,)), sem, sem, sem, sem((NZ,)), sem, sem, sem, sem((4,)), sem, sem,
            sem, sem((2, 4, 2)), sem, sem, sem, sem, sem, sem, sem, sem, sem,
        ],
        compiler_params=pltpu.CompilerParams(
            collective_id=0, has_side_effects=True, vmem_limit_bytes=60 * 1024 * 1024
        ),
    )(
        rotated_slot.reshape(16, 128), selected.T, query_weight, key_weight.T, value_weight.T,
        particles.reshape(128, PIECE, D), out_weight, up_weight, down_weight,
    )
    return result.reshape(512, D)


def solution(mesh):
    in_specs = (
        P("balls", None), P(None, "heads"), P(None, "heads"), P(None, "heads"),
        P(), P(), P(), P(), P(),
    )
    out_specs = P(("balls", "heads"), None)
    return jax.shard_map(
        on_device, mesh=mesh, in_specs=in_specs, out_specs=out_specs, check_vma=False
    )
```

```python
import functools
import math

import jax
import jax.numpy as jnp
from jax import lax
from jax.experimental import pallas as pl
from jax.experimental.pallas import tpu as pltpu
from jax.sharding import PartitionSpec as P

HEAD = 32
BALL = 256
LEAF = 64
TOPK = 3
NX, NY, NZ, NC = 4, 4, 8, 2
NS = NY * NC
PIECE = LEAF // NX
D = 512
FF = 2048
SCALE = math.log2(math.e) / math.sqrt(HEAD)
NT = (((1,), (1,)), ((), ()))
Z_ORDER = (4, 5, 3, 6, 2, 7, 1)


def rms_rows(matrix):
    wide = matrix.astype(jnp.float32)
    return (wide * lax.rsqrt(jnp.mean(wide * wide, axis=-1, keepdims=True) + 1e-05)).astype(
        jnp.bfloat16
    )


def dot32(left, right, dims=None):
    if dims is None:
        return jnp.dot(left, right, preferred_element_type=jnp.float32)
    return lax.dot_general(left, right, dims, preferred_element_type=jnp.float32)


def kernel(
    rs_hbm, sel_hbm, wq_hbm, wk_hbm, wv_hbm, p_hbm, wo_hbm, up_hbm, down_hbm, out_any,
    out_ref,    rs_ref, sel_ref, wq_ref, p_ref, wo_ref, up_ref, down_ref, w_all,
    tab_v, tab_a, tab_b,
    leaf_stage, leaf_mid, leaf_recv, rotq, q_stage, q_recv, rres,
    k_own, k_p1, k_p2, k_p3, k_m1, k_m2, k_m3, k_4,
    v_own, v_p1, v_p2, v_p3, v_m1, v_m2, v_m3, v_4,
    sel_stage, sel_k, sel_v, pool_own, pool_z, pool_all,
    k_a, vt_a, k_b, values, counts, tops, queries, score_buf, att_st, att_recv,
    load_sem, ws, wr, lzs, lzr, lss, lsr, xs, xr, rs, rr,
    ags, agr, sss, ssr_k, ssr_v, pzs, pzr, pss, psr, ats, atr,
):
    b = lax.axis_index("balls")
    h = lax.axis_index("heads")
    y = b // (NZ * NC)
    z = (b // NC) % NZ
    c = b % NC
    k = y * NC + c

    def z_peer(r):
        return {"balls": (y * NZ + (z + r) % NZ) * NC + c, "heads": h}

    def s_peer(o):
        kk = (k + o) % NS
        return {"balls": ((kk // NC) * NZ + z) * NC + kk % NC, "heads": h}

    def x_peer(o):
        return {"balls": b, "heads": (h + o) % NX}

    def remote(src, dst, send, recv, peer):
        return pltpu.make_async_remote_copy(
            src_ref=src, dst_ref=dst, send_sem=send, recv_sem=recv,
            device_id=peer, device_id_type=pl.DeviceIdType.MESH,
        )

    def all_sent(bulk, send):
        remote(bulk, bulk, send, send, x_peer(1)).wait_send()

    def all_here(bulk, recv):
        remote(bulk, bulk, recv, recv, x_peer(1)).wait_recv()

    barrier = pltpu.get_barrier_semaphore()

    @pl.loop(1, NZ)
    def _(r):
        pl.semaphore_signal(barrier, 1, device_id=z_peer(r))

    @pl.loop(1, NS)
    def _(o):
        pl.semaphore_signal(barrier, 1, device_id=s_peer(o))

    @pl.loop(1, NX)
    def _(o):
        pl.semaphore_signal(barrier, 1, device_id=x_peer(o))

    small = [
        pltpu.make_async_copy(rs_hbm, rs_ref, load_sem.at[6]),
        pltpu.make_async_copy(sel_hbm, sel_ref, load_sem.at[7]),
        pltpu.make_async_copy(wq_hbm, wq_ref, load_sem.at[8]),
        pltpu.make_async_copy(wk_hbm, w_all.at[h, pl.ds(128, HEAD)], load_sem.at[9]),
        pltpu.make_async_copy(wv_hbm, w_all.at[h, pl.ds(160, HEAD)], load_sem.at[10]),
    ]
    load_p = pltpu.make_async_copy(p_hbm, p_ref, load_sem.at[0])
    small[0].start()
    load_p.start()
    for load in small[1:]:
        load.start()
    loads = [
        pltpu.make_async_copy(wo_hbm, wo_ref, load_sem.at[1]),
        pltpu.make_async_copy(up_hbm, up_ref, load_sem.at[2]),
        pltpu.make_async_copy(down_hbm, down_ref, load_sem.at[3]),
    ]

    def iota(shape, axis):
        return lax.broadcasted_iota(jnp.int32, shape, axis)

    def slot(dev):
        return (((dev >> 4) * NC + (dev & 1)) << 3) + ((dev >> 1) & 7)

    def device(kk, zz):
        return (((kk >> 1) << 3) + zz) * NC + (kk & 1)

    def table(parts, at, target, which):
        used = sum(part.shape[0] for part in parts)
        if used < 128:
            parts = parts + [jnp.zeros((128 - used, 128), jnp.int32)]
        square = jnp.concatenate(parts, axis=0)
        tab_v[pl.ds(8 * at, 8)] = jnp.broadcast_to(
            jnp.max(square.T, axis=0, keepdims=True) & 63, (8, 128)
        )
        copy = pltpu.make_async_copy(tab_v.at[pl.ds(8 * at, 8)], target, load_sem.at[which])
        copy.start()
        return copy

    i64, lane64 = iota((64, 128), 0), iota((64, 128), 1)
    small[0].wait()
    own_row = rs_ref[pl.ds(b // 4, 1), :]
    found = ((own_row >> 5) == device(i64 & 7, i64 >> 3)) & ((lane64 >> 5) == b % 4)
    send = jnp.where(found, lane64 & 31, 0)
    table_a = table([send], 0, tab_a, 4)

    def selected_tables():
        place, lane = iota((32, 128), 0) + b * 32, iota((32, 128), 1)
        take = jnp.zeros((32, 128), jnp.int32)
        for row in range(16):
            found = rs_ref[pl.ds(row, 1), :] == place
            take = jnp.maximum(take, jnp.where(found, slot(row * 4 + (lane >> 5)), 0))
        i, ball = iota((64, 512), 0), iota((64, 512), 1)
        reader = (ball >> 3) == device(i & 7, z)
        origin = (y * NZ + (i >> 3)) * NC + c
        e, ball_e = iota((32, 512), 0), iota((32, 512), 1)
        give = jnp.zeros((64, 512), jnp.int32)
        fetch = jnp.zeros((32, 512), jnp.int32)
        for t in range(TOPK):
            pick = sel_ref[pl.ds(t, 1), :]
            give = jnp.maximum(give, jnp.where(reader & ((pick >> 3) == origin), pick & 7, 0))
            mine = (ball_e - b * 8) * TOPK + t == e
            fetch = jnp.maximum(fetch, jnp.where(mine, slot(pick >> 3), 0))
        give = functools.reduce(jnp.maximum, [give[:, 128 * q : 128 * q + 128] for q in range(4)])
        fetch = functools.reduce(jnp.maximum, [fetch[:, 128 * q : 128 * q + 128] for q in range(4)])
        return table([give, take, fetch], 1, tab_b, 5)

    load_p.wait()
    table_a.wait()

    @pl.loop(0, NZ)
    def _(zd):
        for kk in range(NS):
            leaf_stage[zd, kk] = p_ref[tab_a[0, zd * NS + kk] * NX + h]

    leaf_mid[z] = leaf_stage[z]
    for load in loads:
        load.start()
    for load in small[1:]:
        load.wait()
    w_all[h, pl.ds(0, 128)] = wq_ref[...].astype(jnp.float32).T.astype(jnp.bfloat16)
    table_b = selected_tables()
    pl.semaphore_wait(barrier, (NZ - 1) + (NS - 1) + (NX - 1))

    def leaf_z(r):
        return remote(
            leaf_stage.at[(z + r) % NZ], leaf_mid.at[z], lzs, lzr.at[r], z_peer(r)
        )

    for r in Z_ORDER:
        leaf_z(r).start()

    def weights(o):
        return remote(w_all.at[h], w_all.at[h], ws, wr, x_peer(o))

    @pl.loop(1, NX)
    def _(o):
        weights(o).start()

    ones8 = jnp.ones((8, BALL), jnp.bfloat16)
    row8 = iota((8, 2 * HEAD), 0)

    def own_ball(i, pooled):
        rows = p_ref[pl.ds(i * 16, 16)].reshape(BALL, D)
        kvt = dot32(w_all[h, pl.ds(128, 2 * HEAD)], rms_rows(rows), NT).astype(jnp.bfloat16)
        k_own[i] = kvt[:HEAD]
        v_own[i] = kvt[HEAD:]
        total = dot32(ones8, kvt, NT) * (1.0 / math.sqrt(BALL))
        return jnp.where(row8 == i, total.astype(jnp.bfloat16).astype(jnp.float32), pooled)

    pooled = lax.fori_loop(0, 8, own_ball, jnp.zeros((8, 2 * HEAD), jnp.float32))
    pool_own[...] = jnp.concatenate([pooled, jnp.zeros((8, 2 * HEAD), jnp.float32)], axis=1)

    def pool_to_z(r):
        return remote(pool_own, pool_z.at[z], pzs, pzr, z_peer(r))

    @pl.loop(1, NZ)
    def _(r):
        pool_to_z(r).start()

    rings = (
        ((k_own, k_p1, k_p2, k_p3, k_4), (k_own, k_m1, k_m2, k_m3, k_4)),
        ((v_own, v_p1, v_p2, v_p3, v_4), (v_own, v_m1, v_m2, v_m3, v_4)),
    )

    def hop(way, step, part):
        return remote(
            rings[part][way][step], rings[part][way][step + 1],
            ags, agr.at[way, step, part], z_peer(1 if way == 0 else NZ - 1),
        )

    for part in range(2):
        hop(0, 0, part).start()
        hop(1, 0, part).start()

    pool_z[z] = pool_own[...]

    table_b.wait()

    def forward(part, source, r):
        zs = (z + NZ - r) % NZ
        first = part * 64
        landing, arrived = ((sel_k, ssr_k), (sel_v, ssr_v))[part]

        @pl.loop(0, NS)
        def _(kk):
            sel_stage[first + r * NS + kk] = source[tab_b[0, zs * NS + kk]]

        landing[k * NZ + zs] = sel_stage[first + r * NS + k]

        @pl.loop(1, NS)
        def _(o):
            remote(
                sel_stage.at[first + r * NS + (k + o) % NS], landing.at[k * NZ + zs],
                sss, arrived, s_peer(o),
            ).start()

    def relay(step, part):
        for way in range(2):
            hop(way, step - 1, part).wait_recv()
            if step < 3 or part == way:
                hop(way, step, part).start()
        forward(part, rings[part][0][step], step)
        forward(part, rings[part][1][step], NZ - step)

    forward(0, k_own, 0)
    forward(1, v_own, 0)

    for i in range(2):
        vt_a[i, pl.ds(HEAD, HEAD), :] = jnp.ones((HEAD, 3 * BALL), jnp.bfloat16)

    def place(i, block, key_t, value_t):
        at = pl.ds(block * BALL, key_t.shape[1])
        k_a[i, at, :] = key_t.astype(jnp.float32).T.astype(jnp.bfloat16)
        vt_a[i, pl.ds(0, HEAD), at] = value_t.astype(jnp.bfloat16)

    def leaf_s(r, o):
        zs = (z + NZ - r) % NZ
        kk = (k + o) % NS
        return remote(
            leaf_mid.at[zs, kk], leaf_recv.at[k * NZ + zs], lss, lsr, s_peer(o)
        )

    for r in (0,) + Z_ORDER:
        if r > 0:
            leaf_z(r).wait_recv()

        @pl.loop(1, NS)
        def _(o):
            leaf_s(r, o).start()

        zs = (z + NZ - r) % NZ
        leaf_recv[k * NZ + zs] = leaf_mid[zs, k]

    def pool_to_s(o):
        return remote(pool_z, pool_all.at[k], pss, psr, s_peer(o))

    all_here(pool_z.at[pl.ds(0, NZ - 1)], pzr)

    @pl.loop(1, NS)
    def _(o):
        pool_to_s(o).start()

    pool_all[k] = pool_z[...]

    relay(1, 0)

    all_here(w_all.at[pl.ds(0, NX - 1)], wr)
    all_here(leaf_recv.at[pl.ds(0, NZ * (NS - 1))], lsr)

    def qkv_x(o, q):
        return remote(
            q_stage.at[(h + o) % NX, q], q_recv.at[h, q], xs, xr.at[q], x_peer(o)
        )

    def project(q):
        for s in range(8):
            rotq[q * 8 + s] = leaf_recv[tab_b[0, 64 + q * 8 + s]]
        rows = rms_rows(rotq[pl.ds(q * 8, 8)].reshape(128, D))
        for g in range(NX):
            q_stage[g, q] = dot32(w_all[g], rows, NT).astype(jnp.bfloat16)
        for o in (2, 1, 3):
            qkv_x(o, q).start()
        q_recv[h, q] = q_stage[h, q]

    def project_two(first):
        @pl.loop(first, first + 2)
        def _(q):
            project(q)

    project_two(0)
    relay(1, 1)
    project_two(2)
    relay(2, 0)

    def resid_x(o):
        return remote(
            rotq.at[pl.ds(((h + o) % NX) * 8, 8)], rres.at[h], rs, rr, x_peer(o)
        )

    rres[h] = rotq[pl.ds(h * 8, 8)]
    eye = (iota((2 * HEAD, 128), 0) == iota((2 * HEAD, 128), 1)).astype(jnp.bfloat16)

    all_here(pool_all.at[pl.ds(0, NS - 1)], psr)

    pool_rows = pool_all[...].reshape(2 * BALL, 128).astype(jnp.bfloat16)
    pool_t = dot32(eye, pool_rows, NT)
    for i in range(2):
        place(i, 1, pool_t[:HEAD], pool_t[HEAD:])

    left = iota((128 + 2 * HEAD, 128), 1) < 64

    def transposed_rows(pair, i):
        tiles = [q_recv[g, pair] for g in range(NX)]
        rolled = [pltpu.roll(tile.astype(jnp.float32), 64, 1).astype(jnp.bfloat16) for tile in tiles]
        if i == 0:
            halves = [jnp.where(left, tiles[g], rolled[g + 1]) for g in (0, 2)]
        else:
            halves = [jnp.where(left, rolled[g], tiles[g + 1]) for g in (0, 2)]
        return jnp.concatenate(halves, axis=1)

    blocks = [pl.ds(BALL * t, BALL) for t in range(3)]

    def run_heads(count, keys, vt, query, start, finish):
        def scores(u, t, top):
            score = dot32(keys(u, t), query(u))
            score_buf[u % 2, blocks[t], :] = score
            part = jnp.max(score.reshape(32, 8, BALL), axis=0)
            return part if top is None else jnp.maximum(top, part)

        upcoming = None
        for t in range(3):
            upcoming = scores(0, t, upcoming)
        for u in range(count):
            top = jnp.max(upcoming, axis=0, keepdims=True)
            before = start(u)
            if before is not None:
                top = jnp.maximum(top, before)
            upcoming, result = None, None
            for t in range(3):
                if u < count - 1:
                    upcoming = scores(u + 1, t, upcoming)
                weight = jnp.exp2((score_buf[u % 2, blocks[t], :] - top) * SCALE)
                part = dot32(vt(u, t), weight.astype(jnp.bfloat16))
                result = part if result is None else result + part
            finish(u, result[:HEAD], result[HEAD:], top, before)

    def attend_own(pair):
        for i in range(2):
            rows = transposed_rows(pair, i)
            queries[pair * 2 + i] = rows[:128]
            place(i, 0, rows[128:160], rows[160:])

        def query(u):
            return queries[pair * 2 + u // 4, pl.ds(HEAD * (u % 4), HEAD)]

        def finish(u, value, count, top, before):
            ball, j = pair * 2 + u // 4, u % 4
            values[ball, pl.ds(HEAD * j, HEAD)] = value
            counts[ball, pl.ds(HEAD * j, HEAD)] = count
            tops[ball, pl.ds(j, 1)] = top

        run_heads(
            8, lambda u, t: k_a[u // 4, blocks[t], :], lambda u, t: vt_a[u // 4, :, blocks[t]],
            query, lambda u: None, finish,
        )

    def attend_selected():
        ones = jnp.ones((HEAD, BALL), jnp.bfloat16)
        balls = [((h + 1 + n // 2) % NX) * 2 + n % 2 for n in range(8)]

        def keys(u, t):
            return k_b[balls[u // 4], blocks[t], :]

        def value_rows(u, t):
            at = tab_b[0, 96 + balls[u // 4] * TOPK + t]
            return jnp.concatenate([sel_v[at], ones], axis=0)

        def query(u):
            return queries[balls[u // 4], pl.ds(HEAD * (u % 4), HEAD)]

        def start(u):
            return tops[balls[u // 4], pl.ds(u % 4, 1)]

        parts = []

        def finish(u, value, count, top, before):
            n, at = u // 4, pl.ds(HEAD * (u % 4), HEAD)
            scale = jnp.exp2((before - top) * SCALE)
            value = value + values[balls[n], at] * scale
            parts.append(value / (count + counts[balls[n], at] * scale))
            if u % 4 == 3:
                att_st[balls[n]] = jnp.concatenate(parts[u - 3 :], axis=0).T.astype(jnp.bfloat16)
                if n < 6:
                    att_x(1 + n // 2, n % 2).start()

        run_heads(32, keys, value_rows, query, start, finish)

    def own_pair(pair):
        all_here(q_stage.at[0, pl.ds(0, NX - 1)], xr.at[pair])
        attend_own(pair)

    relay(2, 1)

    @pl.loop(0, NX)
    def _(pair):
        own_pair(pair)

        @pl.when(pair == 0)
        def _():
            relay(3, 0)

        @pl.when(pair == 1)
        def _():
            relay(3, 1)

            @pl.loop(1, NX)
            def _(o):
                resid_x(o).start()

        @pl.when(pair == 2)
        def _():
            hop(0, 3, 0).wait_recv()
            forward(0, k_4, 4)

    hop(1, 3, 1).wait_recv()
    forward(1, v_4, 4)
    all_here(sel_k.at[pl.ds(0, NZ * (NS - 1))], ssr_k)

    @pl.loop(0, 8)
    def _(ball):
        for t in range(TOPK):
            key_t = sel_k[tab_b[0, 96 + ball * TOPK + t]]
            k_b[ball, blocks[t], :] = key_t.astype(jnp.float32).T.astype(jnp.bfloat16)

    all_here(sel_v.at[pl.ds(0, NZ * (NS - 1))], ssr_v)

    def att_x(o, i):
        return remote(
            att_st.at[((h + o) % NX) * 2 + i], att_recv.at[h, i], ats, atr, x_peer(o)
        )

    attend_selected()
    att_recv[h] = att_st[pl.ds(h * 2, 2)]

    for load in loads:
        load.wait()

    all_here(rres.at[pl.ds(0, NX - 1)], rr)
    all_here(att_st.at[pl.ds(0, 2 * (NX - 1))], atr)
    both = [(i, g) for i in range(2) for g in range(NX)]
    merged = jnp.concatenate(
        [jnp.concatenate([att_recv[g, i] for g in range(NX)], axis=1) for i in range(2)], axis=0
    )
    base = jnp.concatenate([rres[g, pl.ds(i * 4, 4)].reshape(64, D) for i, g in both], axis=0)
    resid = (base.astype(jnp.float32) + dot32(merged, wo_ref[...])).astype(jnp.bfloat16)
    mlp_in = rms_rows(resid)

    def hidden(f, total):
        cols = pl.ds(pl.multiple_of(f * 512, 512), 512)
        inner = jax.nn.gelu(dot32(mlp_in, up_ref[:, cols])).astype(jnp.bfloat16)
        return total + dot32(inner, down_ref[cols, :])

    done = lax.fori_loop(0, FF // 512, hidden, resid.astype(jnp.float32), unroll=4)
    done = done.astype(jnp.bfloat16).reshape(2, NX, 4, PIECE, D)
    for i, g in both:
        for s in range(4):
            out_ref[i, s, g] = done[i, g, s]
    deliver = pltpu.make_async_copy(out_ref, out_any, load_sem.at[0])
    deliver.start()

    deliver.wait()
    all_sent(leaf_stage.at[pl.ds(0, NZ - 1)], lzs)
    all_sent(leaf_recv.at[pl.ds(0, NZ * (NS - 1))], lss)
    all_sent(pool_z.at[pl.ds(0, NZ - 1)], pzs)
    all_sent(pool_all.at[pl.ds(0, NS - 1)], pss)
    all_sent(w_all.at[pl.ds(0, NX - 1)], ws)
    all_sent(q_stage.at[pl.ds(0, NX - 1)], xs)
    all_sent(rres.at[pl.ds(0, NX - 1)], rs)
    all_sent(att_st.at[pl.ds(0, 2 * (NX - 1))], ats)
    all_sent(sel_stage.at[pl.ds(0, 2 * 7 * NS)], ags)
    all_sent(sel_stage.at[pl.ds(0, 2 * NZ * (NS - 1))], sss)


def on_device(
    particles, query_weight, key_weight, value_weight, out_weight, up_weight, down_weight,
    rotated_slot, selected,
):
    bf, f32 = jnp.bfloat16, jnp.float32
    hbm = pl.BlockSpec(memory_space=pl.ANY)
    sem = pltpu.SemaphoreType.DMA
    ball_rows = pltpu.VMEM((8, HEAD, BALL), bf)
    result = pl.pallas_call(
        kernel,
        name="layer",
        out_shape=pltpu.VMEM((2, 4, NX, PIECE, D), bf),
        in_specs=[hbm] * 9,
        out_specs=hbm,
        scratch_shapes=[
            pltpu.VMEM((2, 4, NX, PIECE, D), bf),
            pltpu.VMEM((16, 128), jnp.int32), pltpu.VMEM((TOPK, 512), jnp.int32),
            pltpu.VMEM((D, 128), bf), pltpu.VMEM((128, PIECE, D), bf),
            pltpu.VMEM((D, D), bf), pltpu.VMEM((D, FF), bf), pltpu.VMEM((FF, D), bf),
            pltpu.VMEM((NX, 192, D), bf),
            pltpu.VMEM((16, 128), jnp.int32),
            pltpu.SMEM((8, 128), jnp.int32), pltpu.SMEM((8, 128), jnp.int32),
            pltpu.VMEM((NZ, NS, PIECE, D), bf), pltpu.VMEM((NZ, NS, PIECE, D), bf),
            pltpu.VMEM((NS * NZ, PIECE, D), bf), pltpu.VMEM((32, PIECE, D), bf),
            pltpu.VMEM((NX, 4, 192, 128), bf), pltpu.VMEM((NX, 4, 192, 128), bf),
            pltpu.VMEM((NX, 8, PIECE, D), bf),
            *([ball_rows] * 16),
            pltpu.VMEM((2 * NZ * NS, HEAD, BALL), bf),
            pltpu.VMEM((NS * NZ, HEAD, BALL), bf), pltpu.VMEM((NS * NZ, HEAD, BALL), bf),
            pltpu.VMEM((8, 128), f32), pltpu.VMEM((NZ, 8, 128), f32),
            pltpu.VMEM((NS, NZ, 8, 128), f32),
            pltpu.VMEM((2, 3 * BALL, HEAD), bf), pltpu.VMEM((2, 2 * HEAD, 3 * BALL), bf),
            pltpu.VMEM((8, 3 * BALL, HEAD), bf),
            pltpu.VMEM((8, 128, BALL), f32), pltpu.VMEM((8, 128, BALL), f32),
            pltpu.VMEM((8, 8, BALL), f32), pltpu.VMEM((8, 128, BALL), bf),
            pltpu.VMEM((2, 3 * BALL, BALL), f32),
            pltpu.VMEM((8, BALL, 128), bf), pltpu.VMEM((NX, 2, BALL, 128), bf),
            sem((11,)), sem, sem, sem, sem((NZ,)), sem, sem, sem, sem((4,)), sem, sem,
            sem, sem((2, 4, 2)), sem, sem, sem, sem, sem, sem, sem, sem, sem,
        ],
        compiler_params=pltpu.CompilerParams(
            collective_id=0, has_side_effects=True, vmem_limit_bytes=60 * 1024 * 1024
        ),
    )(
        rotated_slot.reshape(16, 128), selected.T, query_weight, key_weight.T, value_weight.T,
        particles.reshape(128, PIECE, D), out_weight, up_weight, down_weight,
    )
    return result.reshape(512, D)


def solution(mesh):
    in_specs = (
        P("balls", None), P(None, "heads"), P(None, "heads"), P(None, "heads"),
        P(), P(), P(), P(), P(),
    )
    out_specs = P(("balls", "heads"), None)
    return jax.shard_map(
        on_device, mesh=mesh, in_specs=in_specs, out_specs=out_specs, check_vma=False
    )
```
